512 devices in a mesh: space: 128 (over x, y, z_hi, core), modes: 4 (over z_lo).
Axes of the slice: x: 4, y: 8, z: 8 (z_hi: 2, z_lo: 4; z = z_hi * 4 + z_lo), core: 2. Of those that a mesh axis runs over, the one named last changes fastest.
Arguments:
- voltage_expansion: float32 [220, 128, 2048], P('modes', 'space'), may hold values from -6 to 6
- current_injection: float32 [220, 128, 2048], P('modes', 'space'), may hold values from -48 to 48
- thermal_state: float32 [220, 128, 2048], P('modes', 'space'), may hold values from -6 to 6
- average_electric_transport: float32 [128, 2048], P('space'), may hold values from 0.5 to 4
- material_zone: int32 [128, 2048], P('space'), may hold values from 0 to 3
- zone_relative_response: float32 [4, 9], replicated, may hold values from 0.02 to 0.12
- polynomial_exponent_rows: int32 [220, 9], replicated, may hold values from 0 to 3, as said below
- quadrature_abscissa_choice: int32 [512, 9], replicated, may hold values from 0 to 4
- quadrature_integer_share: int32 [512], replicated, may hold values from 1 to 1024
Outputs:
- relaxed_voltage: float32 [220, 128, 2048], P('modes', 'space')
- advanced_thermal_state: float32 [220, 128, 2048], P('modes', 'space')
The draws below stay inside these ranges and needn't reach their ends.
Inputs may be any that keep to these rules, and one draw needn't show every extreme that they name: `polynomial_exponent_rows`: the rows are the 220 multi-indices of total degree at most 3 over 9 parameters, each once.
All inputs are finite; a program needn't handle non-finite values.
Results may differ from the reference program's by a relative error of at most 0.0003.
Values sent between devices are 32-bit elements; how exact they have to be, the bound alone decides.
A program may use at most 64 MiB of HBM per device.

```python
import math
import jax
import jax.numpy as jnp
import numpy as np
from jax import lax

NPAR = 9
EXPANSION_TERMS = 220
NQ = 512
NREG = 4
NY = 256
NZ = 8
VOXELS_SLICE = 2048
VOXELS_LEADING = 128


def draw_polynomial_exponent_rows(key, part):
    listing = [[0] * NPAR]
    for first in range(NPAR):
        entry = [0] * NPAR
        entry[first] += 1
        listing.append(entry)
    for first in range(NPAR):
        for second in range(first, NPAR):
            entry = [0] * NPAR
            entry[first] += 1
            entry[second] += 1
            listing.append(entry)
    for first in range(NPAR):
        for second in range(first, NPAR):
            for third in range(second, NPAR):
                entry = [0] * NPAR
                entry[first] += 1
                entry[second] += 1
                entry[third] += 1
                listing.append(entry)
    table = jnp.asarray(np.array(listing, dtype=np.int32))
    order = jax.random.permutation(jax.random.fold_in(key, 7), table.shape[0])
    return table[order].astype(jnp.int32)


def touch_ends(result, own_key, smallest, high):
    place = [jax.random.randint(jax.random.fold_in(own_key, axis), (), 0, length) for axis, length in enumerate(result.shape)]
    longest = result.shape.index(max(result.shape))
    neighbour = place[:longest] + [(place[longest] + 1) % result.shape[longest]] + place[longest + 1:]
    return result.at[tuple(place)].set(smallest).at[tuple(neighbour)].set(high)


def level_of(rng, shape, cuts, least, largest):
    factor_of, own = 1.0, jax.random.fold_in(rng, 6)
    for dim, shards_of in cuts:
        steps = jnp.exp(jax.random.uniform(jax.random.fold_in(own, dim), (shards_of,), jnp.float32, least / len(cuts), largest / len(cuts)))
        factor_of = factor_of * jnp.repeat(steps, shape[dim] // shards_of).reshape([-1 if axis == dim else 1 for axis in range(len(shape))])
    return factor_of


def normal_values(rng, extent, width, reach, shards=(), held_as=jnp.bfloat16):
    gain = level_of(rng, extent, shards, -0.22, 0.18) if shards else 1.0
    entries = jax.random.normal(rng, extent, jnp.float32) * width * gain
    return jnp.minimum(jnp.maximum(entries, -reach), reach).astype(held_as)


def setup_inputs(seed: int = 0) -> dict:
    splits = jax.random.split(jax.random.key(seed), 10)
    return {
        "voltage_expansion": normal_values(splits[0], (EXPANSION_TERMS, VOXELS_LEADING, VOXELS_SLICE), 1.0, 6.0, ((0, 4), (1, 128)), jnp.float32),
        "current_injection": normal_values(splits[1], (EXPANSION_TERMS, VOXELS_LEADING, VOXELS_SLICE), 8.0, 48.0, ((0, 4), (1, 128)), jnp.float32),
        "thermal_state": normal_values(splits[2], (EXPANSION_TERMS, VOXELS_LEADING, VOXELS_SLICE), 1.0, 6.0, ((0, 4), (1, 128)), jnp.float32),
        "average_electric_transport": jnp.clip(jnp.exp(math.log(4.0) - 2.0794415 * jax.random.uniform(splits[3], (VOXELS_LEADING, VOXELS_SLICE), jnp.float32) ** level_of(splits[3], (VOXELS_LEADING, VOXELS_SLICE), ((0, 128),), -0.2, 0.2)), 0.5, 4.0),
        "material_zone": touch_ends(jax.random.randint(splits[4], (VOXELS_LEADING, VOXELS_SLICE), 0, NREG), jax.random.fold_in(splits[4], 1), 0, NREG - 1).astype(jnp.int32),
        "zone_relative_response": jnp.clip(jax.random.uniform(splits[5], (NREG, NPAR), jnp.float32, 0.02, 0.12), 0.02, 0.12),
        "polynomial_exponent_rows": draw_polynomial_exponent_rows(jax.random.fold_in(splits[9], 71), 0),
        "quadrature_abscissa_choice": touch_ends(jax.random.randint(splits[7], (NQ, NPAR), 0, 5), jax.random.fold_in(splits[7], 1), 0, 4).astype(jnp.int32),
        "quadrature_integer_share": touch_ends(jax.random.randint(splits[8], (NQ,), 1, 1025), jax.random.fold_in(splits[8], 1), 1, 1024).astype(jnp.int32),
    }


HERMITE_NODES = (0.0, 1.355626179974266, -1.355626179974266, 2.8569700138728056, -2.8569700138728056)

def neighbours(field):
    column_ids = jnp.arange(field.shape[-1])
    depth_pos = column_ids % NZ
    row_pos = column_ids // NZ
    z_next = jnp.where(depth_pos < NZ - 1, jnp.roll(field, -1, -1), 0.0)
    z_prev = jnp.where(depth_pos > 0, jnp.roll(field, 1, -1), 0.0)
    y_next = jnp.where(row_pos < NY - 1, jnp.roll(field, -NZ, -1), 0.0)
    y_prev = jnp.where(row_pos > 0, jnp.roll(field, NZ, -1), 0.0)
    return (z_next, z_prev, y_next, y_prev)

def diffusion_operator_weights(padded):
    center = padded[..., 1:-1, :]
    z_next, z_prev, y_next, y_prev = neighbours(center)
    return 6.0 * center - padded[..., 2:, :] - padded[..., :-2, :] - z_next - z_prev - y_next - y_prev

def gradient(padded):
    center = padded[..., 1:-1, :]
    z_next, z_prev, y_next, y_prev = neighbours(center)
    along_x = (padded[..., 2:, :] - padded[..., :-2, :]) * 0.5
    along_y = (y_next - y_prev) * 0.5
    along_z = (z_next - z_prev) * 0.5
    return jnp.stack([along_x, along_y, along_z])

def coupling(row_table, col_table):
    offsets = row_table[:, None, :] - col_table[None, :, :]
    differ_count = lax.optimization_barrier(jnp.sum((offsets != 0).astype(jnp.int32), axis=2))
    layers = [jnp.where(differ_count == 0, 1.0, 0.0).astype(jnp.float32)]
    for which_param in range(row_table.shape[1]):
        larger = jnp.maximum(row_table[:, None, which_param], col_table[None, :, which_param]).astype(jnp.float32)
        linked = (jnp.abs(offsets[:, :, which_param]) == 1) & (differ_count == 1)
        layers.append(jnp.where(linked, jnp.sqrt(larger), 0.0).astype(jnp.float32))
    return jnp.stack(layers)

def node_values(quadrature_abscissa_choice):
    node_vals = jnp.zeros(quadrature_abscissa_choice.shape, jnp.float32)
    for which_node in range(5):
        node_vals = node_vals + jnp.where(quadrature_abscissa_choice == which_node, HERMITE_NODES[which_node], 0.0)
    return node_vals

def basis_values(polynomial_exponent_rows, node_vals):
    poly_terms = [jnp.ones_like(node_vals), node_vals, (node_vals * node_vals - 1.0) / jnp.sqrt(2.0), (node_vals * node_vals * node_vals - 3.0 * node_vals) / jnp.sqrt(6.0)]
    basis_vals = jnp.ones((node_vals.shape[0], polynomial_exponent_rows.shape[0]), jnp.float32)
    for which_param in range(polynomial_exponent_rows.shape[1]):
        degree = polynomial_exponent_rows[:, which_param]
        factor = jnp.zeros_like(basis_vals)
        for which_deg in range(4):
            factor = factor + jnp.where(degree[None, :] == which_deg, poly_terms[which_deg][:, which_param][:, None], 0.0)
        basis_vals = basis_vals * factor
    return basis_vals

def border_slices(field):
    return jnp.pad(field, ((0, 0), (1, 1), (0, 0)))

def reference(voltage_expansion, current_injection, thermal_state, average_electric_transport, material_zone, zone_relative_response, polynomial_exponent_rows, quadrature_abscissa_choice, quadrature_integer_share):
    hp = lax.Precision.HIGHEST
    nreg = zone_relative_response.shape[0]
    sens_cell = jnp.zeros((zone_relative_response.shape[1],) + material_zone.shape, jnp.float32)
    for which_region in range(nreg):
        sens_cell = sens_cell + jnp.where(material_zone[None] == which_region, zone_relative_response[which_region][:, None, None], 0.0)
    coeff = jnp.concatenate([jnp.ones((1,) + material_zone.shape, jnp.float32), sens_cell]) * average_electric_transport
    coup = coupling(polynomial_exponent_rows, polynomial_exponent_rows)
    rough = jnp.moveaxis(diffusion_operator_weights(border_slices(voltage_expansion)), 1, 0)
    coeff_planes = jnp.moveaxis(coeff, 1, 0)

    def couple_plane(pair):
        plane_rough, plane_coeff = pair
        mixed = jnp.einsum('mij,jc->mic', coup, plane_rough, precision=hp)
        return lax.optimization_barrier(jnp.sum(plane_coeff[:, None, :] * mixed, axis=0))
    applied = jnp.moveaxis(lax.map(couple_plane, (rough, coeff_planes)), 0, 1)
    relaxed_voltage = voltage_expansion + 0.8 * (current_injection - applied) / (6.0 * average_electric_transport)
    node_vals = node_values(quadrature_abscissa_choice)
    basis_vals = basis_values(polynomial_exponent_rows, node_vals)
    cond_lift = 1.0 + jnp.dot(zone_relative_response, node_vals.T, precision=hp)
    weighted = basis_vals.T * quadrature_integer_share[None, :].astype(jnp.float32) / (512.0 * NQ * EXPANSION_TERMS)
    padded = border_slices(relaxed_voltage)

    def heat_plane(plane):
        window = lax.dynamic_slice_in_dim(padded, plane, 3, 1)
        grads = gradient(window)[:, :, 0, :]
        point_grads = jnp.einsum('qi,kin->kqn', basis_vals, grads, precision=hp)
        plane_cond = lax.dynamic_index_in_dim(average_electric_transport, plane, 0, keepdims=False)
        plane_region = lax.dynamic_index_in_dim(material_zone, plane, 0, keepdims=False)
        spread = jnp.zeros((cond_lift.shape[1], plane_cond.shape[0]), jnp.float32)
        for which_region in range(nreg):
            spread = spread + jnp.where(plane_region[None, :] == which_region, cond_lift[which_region][:, None], 0.0)
        joule_heat = plane_cond * spread * lax.optimization_barrier(jnp.sum(point_grads * point_grads, axis=0))
        return jnp.dot(weighted, joule_heat, precision=hp)
    thermal_expansion_terms = jnp.moveaxis(lax.map(heat_plane, jnp.arange(VOXELS_LEADING)), 0, 1)
    advanced_thermal_state = thermal_state + 0.1 * (thermal_expansion_terms - 1.5 * diffusion_operator_weights(border_slices(thermal_state)))
    return (relaxed_voltage, advanced_thermal_state)
```

```python
import functools
import math

import jax
import jax.numpy as jnp
from jax import lax
from jax.experimental import pallas as pl
from jax.experimental.pallas import tpu as pltpu
from jax.sharding import PartitionSpec as P

MESH = pl.DeviceIdType.MESH
F32 = jnp.float32
BF16 = jnp.bfloat16
NODE_A = 1.355626179974266
NODE_B = 2.8569700138728056
NMODE = 220
NPAR = 9
NQ = 512
NREG = 4
GRP = 55
SLOT = 56
ROWS = 4 * SLOT
KP = 256
MIX = 0.8 / 6.0
COLUMNS = 32
FAR = 100.0


def split(x):
    hi = x.astype(BF16)
    return hi, (x - hi.astype(F32)).astype(BF16)


def kernel(
    v_ref, i_ref, t_ref, avg_ref, zone_ref, zrr_ref, e_ref, n_ref, share_ref,
    rel_out, adv_out,
    sv, su, st, tfix, vc, uc, tc, rel, adv, rough, hxv, hyv, hxr, hyr, hxt, pkv, pkr, ro, ao,
    tmp, ecol, erow, hrow, ncol, basis_t, acat, bcat, wcat, rcat, pmix, gcat, jsum, jcat, lift,
    a_send, a_recv, h_send, h_recv,
):
    s = lax.axis_index("space")
    m = lax.axis_index("modes")
    k = s // 4
    p = s % 4
    z = (p // 2) * 4 + m
    c = p % 2
    b = z * 2 + c

    def at_chip(col, zz, cc):
        return (col * 4 + (zz // 4) * 2 + cc, zz % 4)

    def at_block(col, bb):
        return at_chip(col, bb // 2, bb % 2)

    k_next, k_prev = (k + 1) % COLUMNS, (k + COLUMNS - 1) % COLUMNS
    b_next, b_prev = (b + 1) % 16, (b + 15) % 16
    hops = [(d, cc) for d in (4, 3, 5, 2, 6, 1, 7) for cc in (0, 1)]

    bar = pltpu.get_barrier_semaphore()

    def greet(dev):
        pl.semaphore_signal(bar, inc=1, device_id=dev, device_id_type=MESH)

    for d, cc in hops:
        greet(at_chip(k, (z + d) % 8, cc))
    greet(at_chip(k, z, 1 - c))
    greet(at_chip(k_next, z, c))
    greet(at_chip(k_prev, z, c))

    def remote(src, dst, ssem, rsem, dev):
        cp = pltpu.make_async_remote_copy(
            src, dst, ssem, rsem, device_id=dev, device_id_type=MESH
        )
        cp.start()

    def slot(ref, pp, mm):
        return ref.at[pp, pl.ds(pl.multiple_of(mm * SLOT, 8), SLOT)]

    def send_in(f, src, dst):
        for d, cc in hops:
            z2 = (z + d) % 8
            remote(src.at[z2 * 2 + cc], slot(dst, p, m), a_send.at[f], a_recv.at[f],
                   at_chip(k, z2, cc))
        remote(src.at[z * 2 + 1 - c], slot(dst, p, m), a_send.at[f], a_recv.at[f],
               at_chip(k, z, 1 - c))
        pltpu.make_async_copy(src.at[b], slot(dst, p, m), a_recv.at[f]).start()

    def send_out(f, src, dst):
        for d, cc in hops:
            z2 = (z + d) % 8
            remote(slot(src, (z2 // 4) * 2 + cc, z2 % 4), dst.at[b], a_send.at[f], a_recv.at[f],
                   at_chip(k, z2, cc))
        remote(slot(src, (z // 4) * 2 + 1 - c, m), dst.at[b], a_send.at[f], a_recv.at[f],
               at_chip(k, z, 1 - c))
        pltpu.make_async_copy(slot(src, p, m), dst.at[b], a_recv.at[f]).start()

    def await_all(f, buf):
        pltpu.make_async_copy(buf, buf, a_recv.at[f]).wait()

    def await_sent(f):
        part = sv.at[pl.ds(0, 15)]
        pltpu.make_async_copy(part, part, a_send.at[f]).wait()

    def halo(j, src, dst, dev):
        remote(src, dst, h_send.at[j], h_recv.at[j], dev)

    def await_halo(j, ref):
        pltpu.make_async_copy(ref, ref, h_recv.at[j]).wait()

    def await_halo_sent(j, ref):
        pltpu.make_async_copy(ref, ref, h_send.at[j]).wait()

    for bb in range(16):
        sv[bb, 0:GRP] = v_ref[pl.ds(bb, GRP, stride=16), :]
        sv[bb, GRP:SLOT] = avg_ref[bb : bb + 1, :]
    pl.semaphore_wait(bar, 17)
    send_in(0, sv, vc)
    for bb in range(16):
        gain = MIX / avg_ref[bb : bb + 1, :]
        su[bb, 0:GRP] = sv[bb, 0:GRP] + i_ref[pl.ds(bb, GRP, stride=16), :] * gain
        su[bb, GRP:SLOT] = zone_ref[bb : bb + 1, :].astype(F32)
    send_in(1, su, uc)
    for bb in range(16):
        st[bb, 0:GRP] = t_ref[pl.ds(bb, GRP, stride=16), :]
        st[bb, GRP:SLOT] = jnp.zeros((1, 128), F32)
    send_in(2, st, tc)

    def lanes(rows):
        return lax.broadcasted_iota(jnp.int32, (rows, 128), 1)

    tmp[...] = jnp.zeros((128, 512), F32)
    tmp[0:NPAR, 0:NMODE] = e_ref[...].astype(F32)
    raw = tmp[0:16, 0:256]
    lane = lax.broadcasted_iota(jnp.int32, (16, 256), 1)
    spaced = jnp.full((16, 256), FAR, F32)
    for g in range(4):
        here = (lane >= SLOT * g) & (lane < SLOT * g + GRP)
        spaced = jnp.where(here, raw if g == 0 else pltpu.roll(raw, g, 1), spaced)
    erow[...] = spaced
    tmp[0:16, 0:256] = spaced
    ecol[...] = jnp.transpose(tmp[:, 0:256])

    choice = n_ref[...]
    node = jnp.where(
        choice == 1, NODE_A,
        jnp.where(choice == 2, -NODE_A,
                  jnp.where(choice == 3, NODE_B, jnp.where(choice == 4, -NODE_B, 0.0))))
    tmp[...] = jnp.zeros((128, 512), F32)
    tmp[0:NPAR, :] = node
    hrow[0, 0:NPAR] = node
    hrow[1, 0:NPAR] = (node * node - 1.0) * (1.0 / math.sqrt(2.0))
    hrow[2, 0:NPAR] = (node * node * node - 3.0 * node) * (1.0 / math.sqrt(6.0))
    ncol[...] = jnp.transpose(tmp[...])

    def basis_rows(i, _):
        rows = pl.ds(pl.multiple_of(i * 8, 8), 8)
        acc = jnp.ones((8, NQ), F32)
        for par in range(NPAR):
            e = ecol[rows, par : par + 1]
            f = jnp.where(e == 1.0, hrow[0, par : par + 1, :], 1.0)
            f = jnp.where(e == 2.0, hrow[1, par : par + 1, :], f)
            f = jnp.where(e == 3.0, hrow[2, par : par + 1, :], f)
            acc = acc * f
        basis_t[rows, :] = jnp.where(ecol[rows, 0:1] < 50.0, acc, 0.0)
        return 0

    lax.fori_loop(0, KP // 8, basis_rows, 0)
    hi, lo = split(jnp.transpose(basis_t[...]))
    bcat[:, 0:KP] = hi
    bcat[:, KP : 2 * KP] = hi
    bcat[:, 2 * KP : 3 * KP] = lo
    weight = share_ref[...].astype(F32) * (1.0 / (512.0 * NQ * NMODE))
    hi, lo = split(basis_t[0:ROWS, :] * weight)
    wcat[:, 0:NQ] = hi
    wcat[:, NQ : 2 * NQ] = hi
    wcat[:, 2 * NQ : 3 * NQ] = lo

    def coupling_rows(i, _):
        rows = pl.ds(pl.multiple_of(i * 16, 16), 16)
        apart = jnp.zeros((16, KP), F32)
        acc = [jnp.zeros((16, KP), F32) for _ in range(NREG)]
        for par in range(NPAR):
            ei = ecol[rows, par : par + 1]
            ej = erow[par : par + 1, :]
            diff = jnp.abs(ei - ej)
            larger = jnp.maximum(ei, ej)
            root = jnp.where(larger == 1.0, 1.0,
                             jnp.where(larger == 2.0, math.sqrt(2.0), math.sqrt(3.0)))
            apart = apart + diff
            link = diff * root
            for r in range(NREG):
                acc[r] = acc[r] + zrr_ref[r, par] * link
        for r in range(NREG):
            hi, lo = split(jnp.where(apart == 1.0, acc[r], 0.0))
            out = pl.ds(pl.multiple_of(r * ROWS + i * 16, 16), 16)
            acat[out, 0:KP] = hi
            acat[out, KP : 2 * KP] = hi
            acat[out, 2 * KP : 3 * KP] = lo
        return 0

    lax.fori_loop(0, ROWS // 16, coupling_rows, 0)

    def lift_rows(i, _):
        rows = pl.ds(pl.multiple_of(i * 8, 8), 8)
        acc = [jnp.ones((8, 128), F32) for _ in range(NREG)]
        for par in range(NPAR):
            nd = jnp.broadcast_to(ncol[rows, par : par + 1], (8, 128))
            for r in range(NREG):
                acc[r] = acc[r] + zrr_ref[r, par] * nd
        for r in range(NREG):
            lift[r, rows, :] = acc[r]
        return 0

    lax.fori_loop(0, NQ // 8, lift_rows, 0)

    for part in range(3):
        gcat[part * KP + ROWS : (part + 1) * KP, :] = jnp.zeros((KP - ROWS, 3 * 512), BF16)
        rcat[part * KP + ROWS : (part + 1) * KP, :] = jnp.zeros((KP - ROWS, 512), BF16)

    lane1 = lanes(1)
    depth = lane1 % 8
    z_has_next = depth < 7
    z_has_prev = depth > 0
    low8 = lane1 < 8
    high8 = lane1 >= 120
    k_low = (k > 0).astype(F32)
    k_high = (k < COLUMNS - 1).astype(F32)
    b_low = (b > 0).astype(F32)
    b_high = (b < 15).astype(F32)

    def tfix_block(bb, _):
        cur = st[bb]
        before = st[jnp.maximum(bb - 1, 0)] * (bb > 0).astype(F32)
        after = st[jnp.minimum(bb + 1, 15)] * (bb < 15).astype(F32)
        y_next = jnp.where(high8, pltpu.roll(after, 120, 1), pltpu.roll(cur, 120, 1))
        y_prev = jnp.where(low8, pltpu.roll(before, 8, 1), pltpu.roll(cur, 8, 1))
        z_next = jnp.where(z_has_next, pltpu.roll(cur, 127, 1), 0.0)
        z_prev = jnp.where(z_has_prev, pltpu.roll(cur, 1, 1), 0.0)
        tfix[bb] = cur - 0.15 * (6.0 * cur - y_next - y_prev - z_next - z_prev)
        return 0

    lax.fori_loop(0, 16, tfix_block, 0)

    chunk = 32
    chunks = ROWS // chunk
    octet = lane1 // 8

    def chunk_of(i):
        return pl.ds(pl.multiple_of(i * chunk, chunk), chunk)

    def pack(src, dst):
        def body(i, _):
            rows = chunk_of(i)
            out = jnp.zeros((chunk, 128), F32)
            for q in range(4):
                x = src[q, rows, :]
                out = jnp.where(octet == q, pltpu.roll(x, 8 * q + 8, 1), out)
                out = jnp.where(octet == 4 + q, pltpu.roll(x, 32 + 8 * q, 1), out)
            dst[rows, :] = out
            return 0

        lax.fori_loop(0, chunks, body, 0)

    def y_pair(x, hy, q, rows):
        above = pltpu.roll(hy[1, rows, :] * b_high, 88 - 8 * q, 1)
        below = hy[0, rows, :] * b_low
        if q:
            below = pltpu.roll(below, 128 - 8 * q, 1)
        y_next = jnp.where(high8, above, pltpu.roll(x, 120, 1))
        y_prev = jnp.where(low8, below, pltpu.roll(x, 8, 1))
        return y_next, y_prev

    def z_pair(x):
        z_next = jnp.where(z_has_next, pltpu.roll(x, 127, 1), 0.0)
        z_prev = jnp.where(z_has_prev, pltpu.roll(x, 1, 1), 0.0)
        return z_next, z_prev

    def x_pair(field, hx, q, rows):
        x_next = field[q + 1, rows, :] if q < 3 else hx[1, rows, :] * k_high
        x_prev = field[q - 1, rows, :] if q > 0 else hx[0, rows, :] * k_low
        return x_next, x_prev

    def exchange_x(j, field, hx):
        halo(j, field.at[3], hx.at[0], at_chip(k_next, z, c))
        halo(j + 1, field.at[0], hx.at[1], at_chip(k_prev, z, c))

    def exchange_y(j, pk, hy):
        halo(j, pk, hy.at[0], at_block(k, b_next))
        halo(j + 1, pk, hy.at[1], at_block(k, b_prev))

    await_all(0, vc)
    exchange_x(0, vc, hxv)
    pack(vc, pkv)
    exchange_y(2, pkv, hyv)
    await_halo(0, hxv.at[0])
    await_halo(1, hxv.at[1])
    await_halo(2, hyv.at[0])
    await_halo(3, hyv.at[1])

    def rough_rows(i, _):
        rows = chunk_of(i)
        for q in range(4):
            x = vc[q, rows, :]
            y_next, y_prev = y_pair(x, hyv, q, rows)
            z_next, z_prev = z_pair(x)
            x_next, x_prev = x_pair(vc, hxv, q, rows)
            value = 6.0 * x - x_next - x_prev - z_next - z_prev - y_next - y_prev
            rough[q, rows, :] = value
            hi, lo = split(value)
            base = i * chunk
            cols = slice(128 * q, 128 * q + 128)
            rcat[pl.ds(pl.multiple_of(base, chunk), chunk), cols] = hi
            rcat[pl.ds(pl.multiple_of(base + KP, chunk), chunk), cols] = lo
            rcat[pl.ds(pl.multiple_of(base + 2 * KP, chunk), chunk), cols] = hi
        return 0

    lax.fori_loop(0, chunks, rough_rows, 0)

    def mix_region(r, _):
        rows = pl.ds(pl.multiple_of(r * ROWS, 32), ROWS)
        pmix[rows, :] = jnp.dot(acat[rows, :], rcat[...], preferred_element_type=F32)
        return 0

    lax.fori_loop(0, NREG, mix_region, 0)

    await_all(1, uc)
    zones = [uc[q, GRP : GRP + 1, :] for q in range(4)]
    avgs = [vc[q, GRP : GRP + 1, :] for q in range(4)]

    def relax_rows(i, _):
        rows = chunk_of(i)
        for q in range(4):
            cols = slice(128 * q, 128 * q + 128)
            part = [
                pmix[pl.ds(pl.multiple_of(r * ROWS + i * chunk, chunk), chunk), cols]
                for r in range(NREG)
            ]
            mixed = part[3]
            for r in range(3):
                mixed = jnp.where(zones[q] == float(r), part[r], mixed)
            rel[q, rows, :] = uc[q, rows, :] - MIX * (rough[q, rows, :] + mixed)
        return 0

    lax.fori_loop(0, chunks, relax_rows, 0)
    exchange_x(4, rel, hxr)
    pack(rel, pkr)
    exchange_y(6, pkr, hyr)
    send_out(3, rel, ro)

    def put_grad(i, col, value):
        hi, lo = split(value)
        base = i * chunk
        cols = slice(col, col + 128)
        gcat[pl.ds(pl.multiple_of(base, chunk), chunk), cols] = hi
        gcat[pl.ds(pl.multiple_of(base + KP, chunk), chunk), cols] = lo
        gcat[pl.ds(pl.multiple_of(base + 2 * KP, chunk), chunk), cols] = hi

    def grad_z(i, _):
        rows = chunk_of(i)
        for q in range(4):
            z_next, z_prev = z_pair(rel[q, rows, :])
            put_grad(i, 1024 + 128 * q, z_next - z_prev)
        return 0

    lax.fori_loop(0, chunks, grad_z, 0)

    def at_points(col, half):
        cols = pl.ds(pl.multiple_of(col + half * 256, 256), 256)
        return jnp.dot(bcat[...], gcat[:, cols], preferred_element_type=F32)

    def half_cols(half):
        return pl.ds(pl.multiple_of(half * 256, 256), 256)

    def points_z(half, _):
        g = at_points(1024, half)
        jsum[:, half_cols(half)] = g * g
        return 0

    lax.fori_loop(0, 2, points_z, 0)

    await_halo(4, hxr.at[0])
    await_halo(5, hxr.at[1])
    await_halo(6, hyr.at[0])
    await_halo(7, hyr.at[1])

    def grad_xy(i, _):
        rows = chunk_of(i)
        for q in range(4):
            y_next, y_prev = y_pair(rel[q, rows, :], hyr, q, rows)
            x_next, x_prev = x_pair(rel, hxr, q, rows)
            put_grad(i, 128 * q, x_next - x_prev)
            put_grad(i, 512 + 128 * q, y_next - y_prev)
        return 0

    lax.fori_loop(0, chunks, grad_xy, 0)

    def points_xy(half, _):
        cols = half_cols(half)
        g = at_points(0, half)
        jsum[:, cols] = jsum[:, cols] + g * g
        g = at_points(512, half)
        jsum[:, cols] = jsum[:, cols] + g * g
        return 0

    lax.fori_loop(0, 2, points_xy, 0)

    await_all(2, tc)
    exchange_x(8, tc, hxt)

    def joule_rows(i, _):
        rows = chunk_of(i)
        for q in range(4):
            gain = lift[3, rows, :]
            for r in range(3):
                gain = jnp.where(zones[q] == float(r), lift[r, rows, :], gain)
            cols = slice(128 * q, 128 * q + 128)
            hi, lo = split(jsum[rows, cols] * gain)
            base = i * chunk
            jcat[pl.ds(pl.multiple_of(base, chunk), chunk), cols] = hi
            jcat[pl.ds(pl.multiple_of(base + NQ, chunk), chunk), cols] = lo
            jcat[pl.ds(pl.multiple_of(base + 2 * NQ, chunk), chunk), cols] = hi
        return 0

    lax.fori_loop(0, NQ // chunk, joule_rows, 0)

    def heat_half(half, _):
        cols = half_cols(half)
        pmix[0:ROWS, cols] = jnp.dot(wcat[...], jcat[:, cols], preferred_element_type=F32)
        return 0

    lax.fori_loop(0, 2, heat_half, 0)
    await_halo(8, hxt.at[0])
    await_halo(9, hxt.at[1])

    def adv_rows(i, _):
        rows = chunk_of(i)
        for q in range(4):
            t_next, t_prev = x_pair(tc, hxt, q, rows)
            scale = avgs[q] * 0.025
            adv[q, rows, :] = (
                pmix[rows, 128 * q : 128 * q + 128] * scale + 0.15 * (t_next + t_prev)
            )
        return 0

    lax.fori_loop(0, chunks, adv_rows, 0)
    send_out(4, adv, ao)

    await_all(3, ro)
    for bb in range(16):
        rel_out[pl.ds(bb, GRP, stride=16), :] = ro[bb, 0:GRP]
    await_all(4, ao)
    for bb in range(16):
        adv_out[pl.ds(bb, GRP, stride=16), :] = ao[bb, 0:GRP] + tfix[bb, 0:GRP]
    for f in range(5):
        await_sent(f)
    for j in range(10):
        await_halo_sent(j, pkv)


def on_device(v, i, t, avg, zone, zrr, exps, choice, share):
    flat = lambda x: x.reshape(GRP * 16, 128)
    vmem = pl.BlockSpec(memory_space=pltpu.VMEM)
    smem = pl.BlockSpec(memory_space=pltpu.SMEM)
    field = pltpu.VMEM((4, ROWS, 128), F32)
    blocks = pltpu.VMEM((16, SLOT, 128), F32)
    pair = pltpu.VMEM((2, ROWS, 128), F32)
    one = pltpu.VMEM((ROWS, 128), F32)
    rel, adv = pl.pallas_call(
        kernel,
        out_shape=[jax.ShapeDtypeStruct((GRP * 16, 128), F32)] * 2,
        in_specs=[vmem] * 5 + [smem] + [vmem] * 3,
        out_specs=[vmem] * 2,
        scratch_shapes=[
            blocks, blocks, blocks, blocks,
            field, field, field, field, field, field,
            pair, pair, pair, pair, pair,
            one, one,
            blocks, blocks,
            pltpu.VMEM((128, 512), F32),
            pltpu.VMEM((256, 128), F32),
            pltpu.VMEM((16, 256), F32),
            pltpu.VMEM((3, 16, NQ), F32),
            pltpu.VMEM((NQ, 128), F32),
            pltpu.VMEM((KP, NQ), F32),
            pltpu.VMEM((NREG * ROWS, 3 * KP), BF16),
            pltpu.VMEM((NQ, 3 * KP), BF16),
            pltpu.VMEM((ROWS, 3 * NQ), BF16),
            pltpu.VMEM((3 * KP, 512), BF16),
            pltpu.VMEM((NREG * ROWS, 512), F32),
            pltpu.VMEM((3 * KP, 3 * 512), BF16),
            pltpu.VMEM((NQ, 512), F32),
            pltpu.VMEM((3 * NQ, 512), BF16),
            pltpu.VMEM((NREG, NQ, 128), F32),
            pltpu.SemaphoreType.DMA((5,)),
            pltpu.SemaphoreType.DMA((5,)),
            pltpu.SemaphoreType.DMA((10,)),
            pltpu.SemaphoreType.DMA((10,)),
        ],
        compiler_params=pltpu.CompilerParams(
            collective_id=0, has_side_effects=True, vmem_limit_bytes=60 << 20
        ),
        name="step",
    )(
        flat(v), flat(i), flat(t), avg.reshape(16, 128), zone.reshape(16, 128), zrr,
        exps.T, choice.T, share.reshape(1, NQ),
    )
    shape = (GRP, 1, 2048)
    return rel.reshape(shape), adv.reshape(shape)


def solution(mesh):
    field = P("modes", "space", None)
    cells = P("space", None)
    return jax.shard_map(
        on_device,
        mesh=mesh,
        in_specs=(field, field, field, cells, cells, P(), P(), P(), P()),
        out_specs=(field, field),
        check_vma=False,
    )
```

```python
import functools
import math

import jax
import jax.numpy as jnp
from jax import lax
from jax.experimental import pallas as pl
from jax.experimental.pallas import tpu as pltpu
from jax.sharding import PartitionSpec as P

MESH = pl.DeviceIdType.MESH
F32 = jnp.float32
BF16 = jnp.bfloat16
NODE_A = 1.355626179974266
NODE_B = 2.8569700138728056
NMODE = 220
NPAR = 9
NQ = 512
NREG = 4
GRP = 55
SLOT = 56
ROWS = 4 * SLOT
KP = 256
MIX = 0.8 / 6.0
COLUMNS = 32
FAR = 100.0


def split(x):
    hi = x.astype(BF16)
    return hi, (x - hi.astype(F32)).astype(BF16)


def kernel(
    v_hbm, i_hbm, t_hbm, avg_hbm, zone_hbm, zrr_ref, e_hbm, n_hbm, share_hbm,
    ro, ao, tfix_out,
    v_ref, i_ref, t_ref, avg_ref, zone_ref, e_ref, n_ref, share_ref,
    sv, su, st, tfix, vc, uc, tc, rel, adv, rough, hxv, hxr, hyr, hxt, sh, yh, pkr,
    tmp, ecol, erow, hrow, ncol, basis_t, acat, bcat, wcat, rcat, pmix, gcat, jsum, jcat, lift,
    in_sem, a_send, a_recv, h_send, h_recv,
):
    s = lax.axis_index("space")
    m = lax.axis_index("modes")
    k = s // 4
    p = s % 4
    z = (p // 2) * 4 + m
    c = p % 2
    b = z * 2 + c

    def at_chip(col, zz, cc):
        return (col * 4 + (zz // 4) * 2 + cc, zz % 4)

    def at_block(col, bb):
        return at_chip(col, bb // 2, bb % 2)

    k_next, k_prev = (k + 1) % COLUMNS, (k + COLUMNS - 1) % COLUMNS
    b_next, b_prev = (b + 1) % 16, (b + 15) % 16
    hops = [(d, cc) for d in (4, 3, 5, 2, 6, 1, 7) for cc in (0, 1)]

    loads = [
        pltpu.make_async_copy(src, dst, in_sem.at[n])
        for n, (src, dst) in enumerate((
            (v_hbm, v_ref), (avg_hbm, avg_ref), (i_hbm, i_ref), (zone_hbm, zone_ref),
            (t_hbm, t_ref), (e_hbm, e_ref), (n_hbm, n_ref), (share_hbm, share_ref)))
    ]
    loads[0].start()
    loads[1].start()

    bar = pltpu.get_barrier_semaphore()

    def greet(dev):
        pl.semaphore_signal(bar, inc=1, device_id=dev, device_id_type=MESH)

    for d, cc in hops:
        greet(at_chip(k, (z + d) % 8, cc))
    greet(at_chip(k, z, 1 - c))
    greet(at_chip(k_next, z, c))
    greet(at_chip(k_prev, z, c))
    for load in loads[2:]:
        load.start()

    def remote(src, dst, ssem, rsem, dev):
        cp = pltpu.make_async_remote_copy(
            src, dst, ssem, rsem, device_id=dev, device_id_type=MESH
        )
        cp.start()

    def slot(ref, pp, mm):
        return ref.at[pp, pl.ds(pl.multiple_of(mm * SLOT, 8), SLOT)]

    early = [hop for hop in hops if hop[0] in (3, 5)]
    late = [hop for hop in hops if hop[0] not in (3, 5)]

    def send_to(f, src, place, some):
        for d, cc in some:
            z2 = (z + d) % 8
            remote(src.at[z2 * 2 + cc], place, a_send.at[f], a_recv.at[f], at_chip(k, z2, cc))

    def send_rest(f, src, place):
        remote(src.at[z * 2 + 1 - c], place, a_send.at[f], a_recv.at[f], at_chip(k, z, 1 - c))
        pltpu.make_async_copy(src.at[b], place, a_recv.at[f]).start()

    def send_out(f, src, dst):
        for d, cc in hops:
            z2 = (z + d) % 8
            remote(slot(src, (z2 // 4) * 2 + cc, z2 % 4), dst.at[b], a_send.at[f], a_recv.at[f],
                   at_chip(k, z2, cc))
        remote(slot(src, (z // 4) * 2 + 1 - c, m), dst.at[b], a_send.at[f], a_recv.at[f],
               at_chip(k, z, 1 - c))
        pltpu.make_async_copy(slot(src, p, m), dst.at[b], a_recv.at[f]).start()

    def await_all(f, buf):
        pltpu.make_async_copy(buf, buf, a_recv.at[f]).wait()

    def await_sent(f, buf):
        part = buf.at[pl.ds(0, 15)]
        pltpu.make_async_copy(part, part, a_send.at[f]).wait()

    def halo(j, src, dst, dev):
        remote(src, dst, h_send.at[j], h_recv.at[j], dev)

    def await_halo(j, ref):
        pltpu.make_async_copy(ref, ref, h_recv.at[j]).wait()

    def await_halo_sent(j, ref):
        pltpu.make_async_copy(ref, ref, h_send.at[j]).wait()

    lane1 = lax.broadcasted_iota(jnp.int32, (1, 128), 1)
    low8 = lane1 < 8
    high8 = lane1 >= 120
    octet = lane1 // 8
    pair16 = lane1 // 16

    loads[0].wait()
    loads[1].wait()
    for bb in range(16):
        sv[bb, 0:GRP] = v_ref[pl.ds(bb, GRP, stride=16), :]
        sv[bb, GRP:SLOT] = avg_ref[bb : bb + 1, :]
    pl.semaphore_wait(bar, 17)
    send_to(0, sv, slot(vc, p, m), hops)
    send_rest(0, sv, slot(vc, p, m))

    def pack_edges(bb, _):
        before = sv[jnp.maximum(bb - 1, 0)] * (bb > 0).astype(F32)
        after = sv[jnp.minimum(bb + 1, 15)] * (bb < 15).astype(F32)
        both = jnp.where(high8, before, after)
        out = jnp.zeros((8, 128), F32)
        for t in range(7):
            moved = pltpu.roll(both[8 * t : 8 * t + 8], (16 * t + 8) % 128, 1)
            out = jnp.where(pair16 == t, moved, out)
        sh[bb] = out
        return 0

    lax.fori_loop(0, 16, pack_edges, 0)
    edge = yh.at[p, pl.ds(pl.multiple_of(m * 8, 8), 8)]
    send_to(5, sh, edge, hops)
    send_rest(5, sh, edge)
    loads[2].wait()
    loads[3].wait()
    for bb in range(16):
        gain = MIX / avg_ref[bb : bb + 1, :]
        su[bb, 0:GRP] = sv[bb, 0:GRP] + i_ref[pl.ds(bb, GRP, stride=16), :] * gain
        su[bb, GRP:SLOT] = zone_ref[bb : bb + 1, :].astype(F32)
    send_to(1, su, slot(uc, p, m), hops)
    send_rest(1, su, slot(uc, p, m))
    loads[4].wait()
    for bb in range(16):
        st[bb, 0:GRP] = t_ref[pl.ds(bb, GRP, stride=16), :]
        st[bb, GRP:SLOT] = jnp.zeros((1, 128), F32)
    send_to(2, st, slot(tc, p, m), early)
    for load in loads[5:]:
        load.wait()

    tmp[...] = jnp.zeros((128, 512), F32)
    tmp[0:NPAR, 0:NMODE] = e_ref[...].astype(F32)
    raw = tmp[0:16, 0:256]
    lane = lax.broadcasted_iota(jnp.int32, (16, 256), 1)
    spaced = jnp.full((16, 256), FAR, F32)
    for g in range(4):
        here = (lane >= SLOT * g) & (lane < SLOT * g + GRP)
        spaced = jnp.where(here, raw if g == 0 else pltpu.roll(raw, g, 1), spaced)
    erow[...] = spaced
    tmp[0:16, 0:256] = spaced
    ecol[...] = jnp.transpose(tmp[:, 0:256])

    choice = n_ref[...]
    node = jnp.where(
        choice == 1, NODE_A,
        jnp.where(choice == 2, -NODE_A,
                  jnp.where(choice == 3, NODE_B, jnp.where(choice == 4, -NODE_B, 0.0))))
    tmp[...] = jnp.zeros((128, 512), F32)
    tmp[0:NPAR, :] = node
    hrow[0, 0:NPAR] = node
    hrow[1, 0:NPAR] = (node * node - 1.0) * (1.0 / math.sqrt(2.0))
    hrow[2, 0:NPAR] = (node * node * node - 3.0 * node) * (1.0 / math.sqrt(6.0))
    ncol[...] = jnp.transpose(tmp[...])

    def basis_rows(i, _):
        rows = pl.ds(pl.multiple_of(i * 8, 8), 8)
        acc = jnp.ones((8, NQ), F32)
        for par in range(NPAR):
            e = ecol[rows, par : par + 1]
            f = jnp.where(e == 1.0, hrow[0, par : par + 1, :], 1.0)
            f = jnp.where(e == 2.0, hrow[1, par : par + 1, :], f)
            f = jnp.where(e == 3.0, hrow[2, par : par + 1, :], f)
            acc = acc * f
        basis_t[rows, :] = jnp.where(ecol[rows, 0:1] < 50.0, acc, 0.0)
        return 0

    lax.fori_loop(0, KP // 8, basis_rows, 0)
    hi, lo = split(jnp.transpose(basis_t[...]))
    bcat[:, 0:KP] = hi
    bcat[:, KP : 2 * KP] = hi
    bcat[:, 2 * KP : 3 * KP] = lo
    weight = share_ref[...].astype(F32) * (1.0 / (512.0 * NQ * NMODE))
    hi, lo = split(basis_t[0:ROWS, :] * weight)
    wcat[:, 0:NQ] = hi
    wcat[:, NQ : 2 * NQ] = hi
    wcat[:, 2 * NQ : 3 * NQ] = lo

    def coupling_rows(i, _):
        rows = pl.ds(pl.multiple_of(i * 16, 16), 16)
        apart = jnp.zeros((16, KP), F32)
        acc = [jnp.zeros((16, KP), F32) for _ in range(NREG)]
        for par in range(NPAR):
            ei = ecol[rows, par : par + 1]
            ej = erow[par : par + 1, :]
            diff = jnp.abs(ei - ej)
            larger = jnp.maximum(ei, ej)
            root = jnp.where(larger == 1.0, 1.0,
                             jnp.where(larger == 2.0, math.sqrt(2.0), math.sqrt(3.0)))
            apart = apart + diff
            link = diff * root
            for r in range(NREG):
                acc[r] = acc[r] + zrr_ref[r, par] * link
        for r in range(NREG):
            hi, lo = split(jnp.where(apart == 1.0, acc[r], 0.0))
            out = pl.ds(pl.multiple_of(r * ROWS + i * 16, 16), 16)
            acat[out, 0:KP] = hi
            acat[out, KP : 2 * KP] = hi
            acat[out, 2 * KP : 3 * KP] = lo
        return 0

    lax.fori_loop(0, ROWS // 16, coupling_rows, 0)

    for part in range(3):
        gcat[part * KP + ROWS : (part + 1) * KP, :] = jnp.zeros((KP - ROWS, 3 * 512), BF16)
        rcat[part * KP + ROWS : (part + 1) * KP, :] = jnp.zeros((KP - ROWS, 512), BF16)

    depth = lane1 % 8
    z_has_next = depth < 7
    z_has_prev = depth > 0
    k_low = (k > 0).astype(F32)
    k_high = (k < COLUMNS - 1).astype(F32)
    b_low = (b > 0).astype(F32)
    b_high = (b < 15).astype(F32)

    chunk = 32
    chunks = ROWS // chunk

    def chunk_of(i):
        return pl.ds(pl.multiple_of(i * chunk, chunk), chunk)

    def y_pair(x, edges):
        y_next = pltpu.roll(jnp.where(low8, edges, x), 120, 1)
        y_prev = pltpu.roll(jnp.where(high8, edges, x), 8, 1)
        return y_next, y_prev

    def z_pair(x):
        z_next = jnp.where(z_has_next, pltpu.roll(x, 127, 1), 0.0)
        z_prev = jnp.where(z_has_prev, pltpu.roll(x, 1, 1), 0.0)
        return z_next, z_prev

    def x_pair(field, hx, q, rows):
        x_next = field[q + 1, rows, :] if q < 3 else hx[1, rows, :] * k_high
        x_prev = field[q - 1, rows, :] if q > 0 else hx[0, rows, :] * k_low
        return x_next, x_prev

    def exchange_x(j, field, hx):
        halo(j, field.at[3], hx.at[0], at_chip(k_next, z, c))
        halo(j + 1, field.at[0], hx.at[1], at_chip(k_prev, z, c))

    def exchange_y(j, pk, hy):
        halo(j, pk, hy.at[0], at_block(k, b_next))
        halo(j + 1, pk, hy.at[1], at_block(k, b_prev))

    await_all(0, vc)
    exchange_x(0, vc, hxv)
    def lift_rows(i, _):
        rows = pl.ds(pl.multiple_of(i * 8, 8), 8)
        acc = [jnp.ones((8, 128), F32) for _ in range(NREG)]
        for par in range(NPAR):
            nd = jnp.broadcast_to(ncol[rows, par : par + 1], (8, 128))
            for r in range(NREG):
                acc[r] = acc[r] + zrr_ref[r, par] * nd
        for r in range(NREG):
            lift[r, rows, :] = acc[r]
        return 0

    lax.fori_loop(0, NQ // 8, lift_rows, 0)

    await_all(5, yh)
    await_halo(0, hxv.at[0])
    await_halo(1, hxv.at[1])

    def rough_group(g, _):
        for q in range(4):
            edges = yh[q, pl.ds(pl.multiple_of(g * 8, 8), 8), :]
            for t in range(7):
                rows = pl.ds(pl.multiple_of(g * SLOT + 8 * t, 8), 8)
                x = vc[q, rows, :]
                y_next, y_prev = y_pair(x, pltpu.roll(edges, 120 - 16 * t, 1))
                z_next, z_prev = z_pair(x)
                x_next, x_prev = x_pair(vc, hxv, q, rows)
                rough[q, rows, :] = (
                    6.0 * x - x_next - x_prev - z_next - z_prev - y_next - y_prev
                )
        return 0

    lax.fori_loop(0, 4, rough_group, 0)

    def rough_rows(i, _):
        for q in range(4):
            hi, lo = split(rough[q, chunk_of(i), :])
            base = i * chunk
            cols = slice(128 * q, 128 * q + 128)
            rcat[pl.ds(pl.multiple_of(base, chunk), chunk), cols] = hi
            rcat[pl.ds(pl.multiple_of(base + KP, chunk), chunk), cols] = lo
            rcat[pl.ds(pl.multiple_of(base + 2 * KP, chunk), chunk), cols] = hi
        return 0

    lax.fori_loop(0, chunks, rough_rows, 0)

    def mix_region(r, _):
        rows = pl.ds(pl.multiple_of(r * ROWS, 32), ROWS)
        pmix[rows, :] = jnp.dot(acat[rows, :], rcat[...], preferred_element_type=F32)
        return 0

    lax.fori_loop(0, NREG, mix_region, 0)

    await_all(1, uc)
    zones = [uc[q, GRP : GRP + 1, :] for q in range(4)]
    avgs = [vc[q, GRP : GRP + 1, :] for q in range(4)]

    def relax_rows(i, _):
        rows = chunk_of(i)
        for q in range(4):
            cols = slice(128 * q, 128 * q + 128)
            part = [
                pmix[pl.ds(pl.multiple_of(r * ROWS + i * chunk, chunk), chunk), cols]
                for r in range(NREG)
            ]
            mixed = part[3]
            for r in range(3):
                mixed = jnp.where(zones[q] == float(r), part[r], mixed)
            rel[q, rows, :] = uc[q, rows, :] - MIX * (rough[q, rows, :] + mixed)
        return 0

    lax.fori_loop(0, chunks, relax_rows, 0)
    exchange_x(4, rel, hxr)

    def pack_rel(i, _):
        out = jnp.zeros((8, 128), F32)
        for j in range(2):
            rows = pl.ds(pl.multiple_of(i * 16 + 8 * j, 8), 8)
            for q in range(4):
                moved = pltpu.roll(rel[q, rows, :], (64 * j + 16 * q + 8) % 128, 1)
                out = jnp.where(pair16 == 4 * j + q, moved, out)
        pkr[pl.ds(pl.multiple_of(i * 8, 8), 8), :] = out
        return 0

    lax.fori_loop(0, ROWS // 16, pack_rel, 0)
    exchange_y(6, pkr, hyr)
    send_to(2, st, slot(tc, p, m), late)
    send_rest(2, st, slot(tc, p, m))
    send_out(3, rel, ro)

    def put_grad(i, col, value):
        hi, lo = split(value)
        base = i * chunk
        cols = slice(col, col + 128)
        gcat[pl.ds(pl.multiple_of(base, chunk), chunk), cols] = hi
        gcat[pl.ds(pl.multiple_of(base + KP, chunk), chunk), cols] = lo
        gcat[pl.ds(pl.multiple_of(base + 2 * KP, chunk), chunk), cols] = hi

    def grad_z(i, _):
        rows = chunk_of(i)
        for q in range(4):
            z_next, z_prev = z_pair(rel[q, rows, :])
            put_grad(i, 1024 + 128 * q, z_next - z_prev)
        return 0

    lax.fori_loop(0, chunks, grad_z, 0)

    def at_points(col, half):
        cols = pl.ds(pl.multiple_of(col + half * 256, 256), 256)
        return jnp.dot(bcat[...], gcat[:, cols], preferred_element_type=F32)

    def half_cols(half):
        return pl.ds(pl.multiple_of(half * 256, 256), 256)

    def points_z(half, _):
        g = at_points(1024, half)
        jsum[:, half_cols(half)] = g * g
        return 0

    lax.fori_loop(0, 2, points_z, 0)

    await_halo(4, hxr.at[0])
    await_halo(5, hxr.at[1])
    await_halo(6, hyr.at[0])
    await_halo(7, hyr.at[1])

    def grad_xy(i, _):
        rows = chunk_of(i)
        packed = []
        for j in range(2):
            tile = pl.ds(pl.multiple_of(i * 16 + 8 * j, 8), 8)
            packed.append(
                jnp.where(octet % 2 == 0, hyr[0, tile, :] * b_low, hyr[1, tile, :] * b_high)
            )
        for q in range(4):
            edges = jnp.concatenate(
                [pltpu.roll(packed[j // 2], (120 - 64 * (j % 2) - 16 * q) % 128, 1)
                 for j in range(4)], axis=0)
            y_next, y_prev = y_pair(rel[q, rows, :], edges)
            x_next, x_prev = x_pair(rel, hxr, q, rows)
            put_grad(i, 128 * q, x_next - x_prev)
            put_grad(i, 512 + 128 * q, y_next - y_prev)
        return 0

    lax.fori_loop(0, chunks, grad_xy, 0)

    def points_xy(half, _):
        cols = half_cols(half)
        g = at_points(0, half)
        jsum[:, cols] = jsum[:, cols] + g * g
        g = at_points(512, half)
        jsum[:, cols] = jsum[:, cols] + g * g
        return 0

    lax.fori_loop(0, 2, points_xy, 0)

    await_all(2, tc)
    exchange_x(8, tc, hxt)

    def joule_rows(i, _):
        rows = chunk_of(i)
        for q in range(4):
            gain = lift[3, rows, :]
            for r in range(3):
                gain = jnp.where(zones[q] == float(r), lift[r, rows, :], gain)
            cols = slice(128 * q, 128 * q + 128)
            hi, lo = split(jsum[rows, cols] * gain)
            base = i * chunk
            jcat[pl.ds(pl.multiple_of(base, chunk), chunk), cols] = hi
            jcat[pl.ds(pl.multiple_of(base + NQ, chunk), chunk), cols] = lo
            jcat[pl.ds(pl.multiple_of(base + 2 * NQ, chunk), chunk), cols] = hi
        return 0

    lax.fori_loop(0, NQ // chunk, joule_rows, 0)

    def heat_half(half, _):
        cols = half_cols(half)
        pmix[0:ROWS, cols] = jnp.dot(wcat[...], jcat[:, cols], preferred_element_type=F32)
        return 0

    lax.fori_loop(0, 2, heat_half, 0)
    await_halo(8, hxt.at[0])
    await_halo(9, hxt.at[1])

    def adv_rows(i, _):
        rows = chunk_of(i)
        for q in range(4):
            t_next, t_prev = x_pair(tc, hxt, q, rows)
            scale = avgs[q] * 0.025
            adv[q, rows, :] = (
                pmix[rows, 128 * q : 128 * q + 128] * scale + 0.15 * (t_next + t_prev)
            )
        return 0

    lax.fori_loop(0, chunks, adv_rows, 0)
    send_out(4, adv, ao)

    def tfix_block(bb, _):
        cur = st[bb]
        before = st[jnp.maximum(bb - 1, 0)] * (bb > 0).astype(F32)
        after = st[jnp.minimum(bb + 1, 15)] * (bb < 15).astype(F32)
        y_next = jnp.where(high8, pltpu.roll(after, 120, 1), pltpu.roll(cur, 120, 1))
        y_prev = jnp.where(low8, pltpu.roll(before, 8, 1), pltpu.roll(cur, 8, 1))
        z_next = jnp.where(z_has_next, pltpu.roll(cur, 127, 1), 0.0)
        z_prev = jnp.where(z_has_prev, pltpu.roll(cur, 1, 1), 0.0)
        tfix[bb] = cur - 0.15 * (6.0 * cur - y_next - y_prev - z_next - z_prev)
        return 0

    lax.fori_loop(0, 16, tfix_block, 0)

    local = pltpu.make_async_copy(tfix, tfix_out, in_sem.at[0])
    local.start()
    await_all(3, ro)
    await_all(4, ao)
    local.wait()
    for f in range(5):
        await_sent(f, sv)
    await_sent(5, sh)
    for j in (0, 1, 4, 5, 8, 9):
        await_halo_sent(j, hxv.at[0])
    for j in (6, 7):
        await_halo_sent(j, pkr)


def assemble(ro, ao, tfix, rel_out, adv_out):
    for bb in range(16):
        rel_out[pl.ds(bb, GRP, stride=16), :] = ro[bb, 0:GRP]
        adv_out[pl.ds(bb, GRP, stride=16), :] = ao[bb, 0:GRP] + tfix[bb, 0:GRP]


def on_device(v, i, t, avg, zone, zrr, exps, choice, share):
    flat = lambda x: x.reshape(GRP * 16, 128)
    vmem = pl.BlockSpec(memory_space=pltpu.VMEM)
    hbm = pl.BlockSpec(memory_space=pl.ANY)
    smem = pl.BlockSpec(memory_space=pltpu.SMEM)
    field = pltpu.VMEM((4, ROWS, 128), F32)
    blocks = pltpu.VMEM((16, SLOT, 128), F32)
    pair = pltpu.VMEM((2, ROWS, 128), F32)
    flats = pltpu.VMEM((GRP * 16, 128), F32)
    packed = pltpu.VMEM((2, ROWS // 2, 128), F32)
    parts = pl.pallas_call(
        kernel,
        out_shape=[jax.ShapeDtypeStruct((16, SLOT, 128), F32)] * 3,
        in_specs=[hbm] * 5 + [smem] + [hbm] * 3,
        out_specs=[hbm] * 3,
        scratch_shapes=[
            flats, flats, flats,
            pltpu.VMEM((16, 128), F32),
            pltpu.VMEM((16, 128), jnp.int32),
            pltpu.VMEM((NPAR, NMODE), jnp.int32),
            pltpu.VMEM((NPAR, NQ), jnp.int32),
            pltpu.VMEM((1, NQ), jnp.int32),
            blocks, blocks, blocks, blocks,
            field, field, field, field, field, field,
            pair, pair, packed, pair,
            pltpu.VMEM((16, 8, 128), F32),
            pltpu.VMEM((4, 32, 128), F32),
            pltpu.VMEM((ROWS // 2, 128), F32),
            pltpu.VMEM((128, 512), F32),
            pltpu.VMEM((256, 128), F32),
            pltpu.VMEM((16, 256), F32),
            pltpu.VMEM((3, 16, NQ), F32),
            pltpu.VMEM((NQ, 128), F32),
            pltpu.VMEM((KP, NQ), F32),
            pltpu.VMEM((NREG * ROWS, 3 * KP), BF16),
            pltpu.VMEM((NQ, 3 * KP), BF16),
            pltpu.VMEM((ROWS, 3 * NQ), BF16),
            pltpu.VMEM((3 * KP, 512), BF16),
            pltpu.VMEM((NREG * ROWS, 512), F32),
            pltpu.VMEM((3 * KP, 3 * 512), BF16),
            pltpu.VMEM((NQ, 512), F32),
            pltpu.VMEM((3 * NQ, 512), BF16),
            pltpu.VMEM((NREG, NQ, 128), F32),
            pltpu.SemaphoreType.DMA((8,)),
            pltpu.SemaphoreType.DMA((6,)),
            pltpu.SemaphoreType.DMA((6,)),
            pltpu.SemaphoreType.DMA((10,)),
            pltpu.SemaphoreType.DMA((10,)),
        ],
        compiler_params=pltpu.CompilerParams(
            collective_id=0, has_side_effects=True, vmem_limit_bytes=60 << 20
        ),
        name="step",
    )(
        flat(v), flat(i), flat(t), avg.reshape(16, 128), zone.reshape(16, 128), zrr,
        exps.T, choice.T, share.reshape(1, NQ),
    )
    rel, adv = pl.pallas_call(
        assemble,
        out_shape=[jax.ShapeDtypeStruct((GRP * 16, 128), F32)] * 2,
        in_specs=[vmem] * 3,
        out_specs=[vmem] * 2,
        name="assemble",
    )(*parts)
    shape = (GRP, 1, 2048)
    return rel.reshape(shape), adv.reshape(shape)


def solution(mesh):
    field = P("modes", "space", None)
    cells = P("space", None)
    return jax.shard_map(
        on_device,
        mesh=mesh,
        in_specs=(field, field, field, cells, cells, P(), P(), P(), P()),
        out_specs=(field, field),
        check_vma=False,
    )
```

```python
import functools
import math

import jax
import jax.numpy as jnp
from jax import lax
from jax.experimental import pallas as pl
from jax.experimental.pallas import tpu as pltpu
from jax.sharding import PartitionSpec as P

MESH = pl.DeviceIdType.MESH
F32 = jnp.float32
BF16 = jnp.bfloat16
NODE_A = 1.355626179974266
NODE_B = 2.8569700138728056
NMODE = 220
NPAR = 9
NQ = 512
NREG = 4
GRP = 55
SLOT = 56
ROWS = 4 * SLOT
KP = 256
MIX = 0.8 / 6.0
COLUMNS = 32
FAR = 100.0


def split(x):
    hi = x.astype(BF16)
    return hi, (x - hi.astype(F32)).astype(BF16)


def kernel(
    v_hbm, i_hbm, t_hbm, avg_hbm, zone_hbm, zrr_hbm, e_hbm, n_hbm, share_hbm,
    rel_out, ao, tfix_out,
    v_ref, i_ref, t_ref, avg_ref, zone_ref, zrr_ref, e_ref, n_ref, share_ref,
    sv, su, st, tfix, vc, uc, tc, rel, adv, rough, ro, hxv, hyv, hxr, hyr, hxt, pkv, pkr,
    tmp, ecol, erow, hrow, ncol, basis_t, acat, bcat, wcat, rcat, pmix, gcat, jsum, jcat, lift,
    in_sem, a_send, a_recv, h_send, h_recv,
):
    s = lax.axis_index("space")
    m = lax.axis_index("modes")
    k = s // 4
    p = s % 4
    z = (p // 2) * 4 + m
    c = p % 2
    b = z * 2 + c

    def at_chip(col, zz, cc):
        return (col * 4 + (zz // 4) * 2 + cc, zz % 4)

    def at_block(col, bb):
        return at_chip(col, bb // 2, bb % 2)

    k_next, k_prev = (k + 1) % COLUMNS, (k + COLUMNS - 1) % COLUMNS
    b_next, b_prev = (b + 1) % 16, (b + 15) % 16
    hops = [(d, cc) for d in (4, 3, 5, 2, 6, 1, 7) for cc in (0, 1)]

    loads = [
        pltpu.make_async_copy(src, dst, in_sem.at[n])
        for n, (src, dst) in enumerate((
            (v_hbm, v_ref), (avg_hbm, avg_ref), (i_hbm, i_ref), (zone_hbm, zone_ref),
            (t_hbm, t_ref), (zrr_hbm, zrr_ref), (e_hbm, e_ref), (n_hbm, n_ref), (share_hbm, share_ref)))
    ]
    loads[0].start()
    loads[1].start()

    for g in range(4):
        tc[:, g * SLOT + GRP : (g + 1) * SLOT] = jnp.zeros((4, 1, 128), F32)

    bar = pltpu.get_barrier_semaphore()

    def greet(dev):
        pl.semaphore_signal(bar, inc=1, device_id=dev, device_id_type=MESH)

    for d, cc in hops:
        greet(at_chip(k, (z + d) % 8, cc))
    greet(at_chip(k, z, 1 - c))
    greet(at_chip(k_next, z, c))
    greet(at_chip(k_prev, z, c))
    for load in loads[2:]:
        load.start()

    def remote(src, dst, ssem, rsem, dev):
        cp = pltpu.make_async_remote_copy(
            src, dst, ssem, rsem, device_id=dev, device_id_type=MESH
        )
        cp.start()

    def slot(ref, pp, mm, size=SLOT):
        return ref.at[pp, pl.ds(pl.multiple_of(mm * SLOT, 8), size)]

    first = [hop for hop in hops if hop[0] in (3, 5)]
    second = [hop for hop in hops if hop[0] in (4, 2, 6)]
    third = [hop for hop in hops if hop[0] in (1, 7)]

    def send_to(f, src, place, some):
        for d, cc in some:
            z2 = (z + d) % 8
            remote(src.at[z2 * 2 + cc, pl.ds(0, place.shape[0])], place, a_send.at[f], a_recv.at[f], at_chip(k, z2, cc))

    def send_rest(f, src, place):
        size = pl.ds(0, place.shape[0])
        remote(src.at[z * 2 + 1 - c, size], place, a_send.at[f], a_recv.at[f],
               at_chip(k, z, 1 - c))
        pltpu.make_async_copy(src.at[b, size], place, a_recv.at[f]).start()

    def send_out(f, src, dst, outer):
        place = dst.at[b, pl.ds(0, GRP)]
        for d in (4, 3, 5, 2, 6, 1, 7, 0):
            z2 = (z + d) % 8
            zh = z2 // 4
            cc = zh if outer else 1 - zh
            if d:
                remote(slot(src, zh * 2 + cc, z2 % 4, GRP), place, a_send.at[f], a_recv.at[f],
                       at_chip(k, z2, cc))
                continue
            block = slot(src, zh * 2 + cc, m, GRP)

            @pl.when(cc == c)
            def _():
                pltpu.make_async_copy(block, place, a_recv.at[f]).start()

            @pl.when(cc != c)
            def _():
                remote(block, place, a_send.at[f], a_recv.at[f], at_chip(k, z, 1 - c))

    def await_all(f, buf):
        if f >= 2:
            buf = buf.at[:, pl.ds(0, 4 * GRP)] if f == 2 else buf.at[:, pl.ds(0, GRP)]
        pltpu.make_async_copy(buf, buf, a_recv.at[f]).wait()

    def await_sent(f, buf):
        part = buf.at[pl.ds(0, 15), pl.ds(0, SLOT if f < 2 else GRP)]
        pltpu.make_async_copy(part, part, a_send.at[f]).wait()

    def halo(j, src, dst, dev):
        remote(src, dst, h_send.at[j], h_recv.at[j], dev)

    def await_halo(j, ref):
        pltpu.make_async_copy(ref, ref, h_recv.at[j]).wait()

    def await_halo_sent(j, ref):
        pltpu.make_async_copy(ref, ref, h_send.at[j]).wait()

    lane1 = lax.broadcasted_iota(jnp.int32, (1, 128), 1)
    low8 = lane1 < 8
    high8 = lane1 >= 120
    octet = lane1 // 8
    pair16 = lane1 // 16

    loads[0].wait()
    loads[1].wait()
    for bb in range(16):
        sv[bb, 0:GRP] = v_ref[pl.ds(bb, GRP, stride=16), :]
        sv[bb, GRP:SLOT] = avg_ref[bb : bb + 1, :]
    pl.semaphore_wait(bar, 17)
    send_to(0, sv, slot(vc, p, m), hops)
    send_rest(0, sv, slot(vc, p, m))

    loads[4].wait()
    for bb in range(16):
        st[bb, 0:GRP] = t_ref[pl.ds(bb, GRP, stride=16), :]
        st[bb, GRP:SLOT] = jnp.zeros((1, 128), F32)
    send_to(2, st, slot(tc, p, m, GRP), first)
    loads[2].wait()
    loads[3].wait()
    for bb in range(16):
        gain = MIX / avg_ref[bb : bb + 1, :]
        su[bb, 0:GRP] = sv[bb, 0:GRP] + i_ref[pl.ds(bb, GRP, stride=16), :] * gain
        su[bb, GRP:SLOT] = zone_ref[bb : bb + 1, :].astype(F32)
    for load in loads[5:]:
        load.wait()

    tmp[...] = jnp.zeros((128, 512), F32)
    tmp[0:NPAR, 0:NMODE] = e_ref[...].astype(F32)
    raw = tmp[0:16, 0:256]
    lane = lax.broadcasted_iota(jnp.int32, (16, 256), 1)
    spaced = jnp.full((16, 256), FAR, F32)
    for g in range(4):
        here = (lane >= SLOT * g) & (lane < SLOT * g + GRP)
        spaced = jnp.where(here, raw if g == 0 else pltpu.roll(raw, g, 1), spaced)
    erow[...] = spaced
    tmp[0:16, 0:256] = spaced
    ecol[...] = jnp.transpose(tmp[:, 0:256])

    choice = n_ref[...]
    node = jnp.where(
        choice == 1, NODE_A,
        jnp.where(choice == 2, -NODE_A,
                  jnp.where(choice == 3, NODE_B, jnp.where(choice == 4, -NODE_B, 0.0))))
    tmp[...] = jnp.zeros((128, 512), F32)
    tmp[0:NPAR, :] = node
    hrow[0, 0:NPAR] = node
    hrow[1, 0:NPAR] = (node * node - 1.0) * (1.0 / math.sqrt(2.0))
    hrow[2, 0:NPAR] = (node * node * node - 3.0 * node) * (1.0 / math.sqrt(6.0))
    ncol[...] = jnp.transpose(tmp[...])

    def basis_rows(i, _):
        rows = pl.ds(pl.multiple_of(i * 8, 8), 8)
        acc = jnp.ones((8, NQ), F32)
        for par in range(NPAR):
            e = ecol[rows, par : par + 1]
            f = jnp.where(e == 1.0, hrow[0, par : par + 1, :], 1.0)
            f = jnp.where(e == 2.0, hrow[1, par : par + 1, :], f)
            f = jnp.where(e == 3.0, hrow[2, par : par + 1, :], f)
            acc = acc * f
        basis_t[rows, :] = jnp.where(ecol[rows, 0:1] < 50.0, acc, 0.0)
        return 0

    lax.fori_loop(0, KP // 8, basis_rows, 0)
    hi, lo = split(jnp.transpose(basis_t[...]))
    bcat[:, 0:KP] = hi
    bcat[:, KP : 2 * KP] = hi
    bcat[:, 2 * KP : 3 * KP] = lo
    weight = share_ref[...].astype(F32) * (1.0 / (512.0 * NQ * NMODE))
    hi, lo = split(basis_t[0:ROWS, :] * weight)
    wcat[:, 0:NQ] = hi
    wcat[:, NQ : 2 * NQ] = hi
    wcat[:, 2 * NQ : 3 * NQ] = lo

    def coupling_rows(i, _):
        rows = pl.ds(pl.multiple_of(i * 16, 16), 16)
        apart = jnp.zeros((16, KP), F32)
        acc = [jnp.zeros((16, KP), F32) for _ in range(NREG)]
        for par in range(NPAR):
            ei = ecol[rows, par : par + 1]
            ej = erow[par : par + 1, :]
            diff = jnp.abs(ei - ej)
            larger = jnp.maximum(ei, ej)
            root = jnp.where(larger == 1.0, 1.0,
                             jnp.where(larger == 2.0, math.sqrt(2.0), math.sqrt(3.0)))
            apart = apart + diff
            link = diff * root
            for r in range(NREG):
                acc[r] = acc[r] + zrr_ref[r, par] * link
        for r in range(NREG):
            hi, lo = split(jnp.where(apart == 1.0, acc[r], 0.0))
            out = pl.ds(pl.multiple_of(r * ROWS + i * 16, 16), 16)
            acat[out, 0:KP] = hi
            acat[out, KP : 2 * KP] = hi
            acat[out, 2 * KP : 3 * KP] = lo
        return 0

    lax.fori_loop(0, ROWS // 16, coupling_rows, 0)

    for part in range(3):
        gcat[part * KP + ROWS : (part + 1) * KP, :] = jnp.zeros((KP - ROWS, 3 * 512), BF16)
        rcat[part * KP + ROWS : (part + 1) * KP, :] = jnp.zeros((KP - ROWS, 512), BF16)

    depth = lane1 % 8
    z_has_next = depth < 7
    z_has_prev = depth > 0
    k_low = (k > 0).astype(F32)
    k_high = (k < COLUMNS - 1).astype(F32)
    b_low = (b > 0).astype(F32)
    b_high = (b < 15).astype(F32)

    chunk = 32
    chunks = ROWS // chunk

    def chunk_of(i):
        return pl.ds(pl.multiple_of(i * chunk, chunk), chunk)

    def y_pair(x, edges):
        y_next = pltpu.roll(jnp.where(low8, edges, x), 120, 1)
        y_prev = pltpu.roll(jnp.where(high8, edges, x), 8, 1)
        return y_next, y_prev

    def z_pair(x):
        z_next = jnp.where(z_has_next, pltpu.roll(x, 127, 1), 0.0)
        z_prev = jnp.where(z_has_prev, pltpu.roll(x, 1, 1), 0.0)
        return z_next, z_prev

    def x_pair(field, hx, q, rows):
        x_next = field[q + 1, rows, :] if q < 3 else hx[1, rows, :] * k_high
        x_prev = field[q - 1, rows, :] if q > 0 else hx[0, rows, :] * k_low
        return x_next, x_prev

    def exchange_x(j, field, hx):
        halo(j, field.at[3], hx.at[0], at_chip(k_next, z, c))
        halo(j + 1, field.at[0], hx.at[1], at_chip(k_prev, z, c))

    def exchange_y(j, pk, hy):
        halo(j, pk, hy.at[0], at_block(k, b_next))
        halo(j + 1, pk, hy.at[1], at_block(k, b_prev))

    await_all(0, vc)
    exchange_x(0, vc, hxv)

    def pack(src, dst):
        def body(i, _):
            for half in range(2):
                out = jnp.zeros((8, 128), F32)
                for j in range(2):
                    rows = pl.ds(pl.multiple_of(i * 32 + 16 * half + 8 * j, 8), 8)
                    for q in range(4):
                        moved = pltpu.roll(src[q, rows, :], (64 * j + 16 * q + 8) % 128, 1)
                        out = jnp.where(pair16 == 4 * j + q, moved, out)
                dst[pl.ds(pl.multiple_of(i * 16 + 8 * half, 8), 8), :] = out
            return 0

        lax.fori_loop(0, ROWS // 32, body, 0, unroll=True)

    def edges_of(hy, i):
        both = []
        for half in range(2):
            tile = pl.ds(pl.multiple_of(i * 16 + 8 * half, 8), 8)
            both.append(
                jnp.where(octet % 2 == 0, hy[0, tile, :] * b_low, hy[1, tile, :] * b_high)
            )
        return [
            jnp.concatenate(
                [pltpu.roll(both[j // 2], (120 - 64 * (j % 2) - 16 * q) % 128, 1)
                 for j in range(4)], axis=0)
            for q in range(4)
        ]

    pack(vc, pkv)
    exchange_y(2, pkv, hyv)
    send_to(1, su, slot(uc, p, m), hops)
    send_rest(1, su, slot(uc, p, m))
    send_to(2, st, slot(tc, p, m, GRP), second)
    send_rest(2, st, slot(tc, p, m, GRP))

    def lift_rows(i, _):
        rows = pl.ds(pl.multiple_of(i * 8, 8), 8)
        acc = [jnp.ones((8, 128), F32) for _ in range(NREG)]
        for par in range(NPAR):
            nd = jnp.broadcast_to(ncol[rows, par : par + 1], (8, 128))
            for r in range(NREG):
                acc[r] = acc[r] + zrr_ref[r, par] * nd
        for r in range(NREG):
            lift[r, rows, :] = acc[r]
        return 0

    lax.fori_loop(0, NQ // 8, lift_rows, 0)

    await_halo(0, hxv.at[0])
    await_halo(1, hxv.at[1])
    await_halo(2, hyv.at[0])
    await_halo(3, hyv.at[1])

    def rough_rows(i, _):
        rows = chunk_of(i)
        edges = edges_of(hyv, i)
        for q in range(4):
            x = vc[q, rows, :]
            y_next, y_prev = y_pair(x, edges[q])
            z_next, z_prev = z_pair(x)
            x_next, x_prev = x_pair(vc, hxv, q, rows)
            value = 6.0 * x - x_next - x_prev - z_next - z_prev - y_next - y_prev
            rough[q, rows, :] = value
            hi, lo = split(value)
            base = i * chunk
            cols = slice(128 * q, 128 * q + 128)
            rcat[pl.ds(pl.multiple_of(base, chunk), chunk), cols] = hi
            rcat[pl.ds(pl.multiple_of(base + KP, chunk), chunk), cols] = lo
            rcat[pl.ds(pl.multiple_of(base + 2 * KP, chunk), chunk), cols] = hi
        return 0

    lax.fori_loop(0, chunks, rough_rows, 0)

    def mix_region(r, _):
        rows = pl.ds(pl.multiple_of(r * ROWS, 32), ROWS)
        pmix[rows, :] = jnp.dot(acat[rows, :], rcat[...], preferred_element_type=F32)
        return 0

    lax.fori_loop(0, NREG, mix_region, 0)

    await_all(1, uc)
    zones = [uc[q, GRP : GRP + 1, :] for q in range(4)]
    avgs = [vc[q, GRP : GRP + 1, :] for q in range(4)]

    def relax_rows(i, _):
        rows = chunk_of(i)
        for q in range(4):
            cols = slice(128 * q, 128 * q + 128)
            part = [
                pmix[pl.ds(pl.multiple_of(r * ROWS + i * chunk, chunk), chunk), cols]
                for r in range(NREG)
            ]
            mixed = part[3]
            for r in range(3):
                mixed = jnp.where(zones[q] == float(r), part[r], mixed)
            rel[q, rows, :] = uc[q, rows, :] - MIX * (rough[q, rows, :] + mixed)
        return 0

    lax.fori_loop(0, chunks, relax_rows, 0)
    exchange_x(4, rel, hxr)
    pack(rel, pkr)
    exchange_y(6, pkr, hyr)
    send_to(2, st, slot(tc, p, m, GRP), third)
    send_out(3, rel, ro, False)
    send_out(3, rel, ro, True)

    def put_grad(i, col, value):
        hi, lo = split(value)
        base = i * chunk
        cols = slice(col, col + 128)
        gcat[pl.ds(pl.multiple_of(base, chunk), chunk), cols] = hi
        gcat[pl.ds(pl.multiple_of(base + KP, chunk), chunk), cols] = lo
        gcat[pl.ds(pl.multiple_of(base + 2 * KP, chunk), chunk), cols] = hi

    def grad_z(i, _):
        rows = chunk_of(i)
        for q in range(4):
            z_next, z_prev = z_pair(rel[q, rows, :])
            put_grad(i, 1024 + 128 * q, z_next - z_prev)
        return 0

    lax.fori_loop(0, chunks, grad_z, 0)

    def at_points(col, half):
        cols = pl.ds(pl.multiple_of(col + half * 256, 256), 256)
        return jnp.dot(bcat[...], gcat[:, cols], preferred_element_type=F32)

    def half_cols(half):
        return pl.ds(pl.multiple_of(half * 256, 256), 256)

    def points_z(half, _):
        g = at_points(1024, half)
        jsum[:, half_cols(half)] = g * g
        return 0

    lax.fori_loop(0, 2, points_z, 0)

    await_halo(4, hxr.at[0])
    await_halo(5, hxr.at[1])
    await_halo(6, hyr.at[0])
    await_halo(7, hyr.at[1])

    def grad_xy(i, _):
        rows = chunk_of(i)
        edges = edges_of(hyr, i)
        for q in range(4):
            y_next, y_prev = y_pair(rel[q, rows, :], edges[q])
            x_next, x_prev = x_pair(rel, hxr, q, rows)
            put_grad(i, 128 * q, x_next - x_prev)
            put_grad(i, 512 + 128 * q, y_next - y_prev)
        return 0

    lax.fori_loop(0, chunks, grad_xy, 0)

    def points_xy(half, _):
        cols = half_cols(half)
        g = at_points(0, half)
        jsum[:, cols] = jsum[:, cols] + g * g
        g = at_points(512, half)
        jsum[:, cols] = jsum[:, cols] + g * g
        return 0

    lax.fori_loop(0, 2, points_xy, 0)

    await_all(2, tc)
    exchange_x(8, tc, hxt)

    def joule_rows(i, _):
        rows = chunk_of(i)
        for q in range(4):
            gain = lift[3, rows, :]
            for r in range(3):
                gain = jnp.where(zones[q] == float(r), lift[r, rows, :], gain)
            cols = slice(128 * q, 128 * q + 128)
            hi, lo = split(jsum[rows, cols] * gain)
            base = i * chunk
            jcat[pl.ds(pl.multiple_of(base, chunk), chunk), cols] = hi
            jcat[pl.ds(pl.multiple_of(base + NQ, chunk), chunk), cols] = lo
            jcat[pl.ds(pl.multiple_of(base + 2 * NQ, chunk), chunk), cols] = hi
        return 0

    lax.fori_loop(0, NQ // chunk, joule_rows, 0)

    def heat_half(half, _):
        cols = half_cols(half)
        pmix[0:ROWS, cols] = jnp.dot(wcat[...], jcat[:, cols], preferred_element_type=F32)
        return 0

    lax.fori_loop(0, 2, heat_half, 0)
    def adv_rows(outer):
        def body(i, _):
            rows = chunk_of(i)
            for q in (0, 3) if outer else (1, 2):
                t_next, t_prev = x_pair(tc, hxt, q, rows)
                scale = avgs[q] * 0.025
                adv[q, rows, :] = (
                    pmix[rows, 128 * q : 128 * q + 128] * scale + 0.15 * (t_next + t_prev)
                )
            return 0

        lax.fori_loop(0, chunks, body, 0)

    adv_rows(False)
    send_out(4, adv, ao, False)
    await_halo(8, hxt.at[0])
    await_halo(9, hxt.at[1])
    adv_rows(True)
    send_out(4, adv, ao, True)

    def tfix_block(bb, _):
        cur = st[bb]
        before = st[jnp.maximum(bb - 1, 0)] * (bb > 0).astype(F32)
        after = st[jnp.minimum(bb + 1, 15)] * (bb < 15).astype(F32)
        y_next = jnp.where(high8, pltpu.roll(after, 120, 1), pltpu.roll(cur, 120, 1))
        y_prev = jnp.where(low8, pltpu.roll(before, 8, 1), pltpu.roll(cur, 8, 1))
        z_next = jnp.where(z_has_next, pltpu.roll(cur, 127, 1), 0.0)
        z_prev = jnp.where(z_has_prev, pltpu.roll(cur, 1, 1), 0.0)
        tfix[bb] = cur - 0.15 * (6.0 * cur - y_next - y_prev - z_next - z_prev)
        return 0

    lax.fori_loop(0, 16, tfix_block, 0)

    local = pltpu.make_async_copy(tfix, tfix_out, in_sem.at[0])
    local.start()
    await_all(3, ro)
    for bb in range(16):
        v_ref[pl.ds(bb, GRP, stride=16), :] = ro[bb, 0:GRP]
    final = pltpu.make_async_copy(v_ref, rel_out, in_sem.at[1])
    final.start()
    await_all(4, ao)
    local.wait()
    final.wait()
    for f in range(5):
        await_sent(f, sv)
    for j in (0, 1, 4, 5, 8, 9):
        await_halo_sent(j, hxv.at[0])
    for j in (2, 3, 6, 7):
        await_halo_sent(j, pkr)


def assemble(rel, ao, tfix, rel_out, adv_out, adv, sem):
    first = pltpu.make_async_copy(rel, rel_out, sem.at[0])
    first.start()
    for bb in range(16):
        adv[pl.ds(bb, GRP, stride=16), :] = ao[bb, 0:GRP] + tfix[bb, 0:GRP]
    second = pltpu.make_async_copy(adv, adv_out, sem.at[1])
    second.start()
    first.wait()
    second.wait()


def on_device(v, i, t, avg, zone, zrr, exps, choice, share):
    flat = lambda x: x.reshape(GRP * 16, 128)
    vmem = pl.BlockSpec(memory_space=pltpu.VMEM)
    hbm = pl.BlockSpec(memory_space=pltpu.HBM)
    free = pl.BlockSpec(memory_space=pl.ANY)
    field = pltpu.VMEM((4, ROWS, 128), F32)
    blocks = pltpu.VMEM((16, SLOT, 128), F32)
    pair = pltpu.VMEM((2, ROWS, 128), F32)
    flats = pltpu.VMEM((GRP * 16, 128), F32)
    edge = pltpu.VMEM((ROWS // 2, 128), F32)
    packed = pltpu.VMEM((2, ROWS // 2, 128), F32)
    parts = pl.pallas_call(
        kernel,
        out_shape=[jax.ShapeDtypeStruct((GRP * 16, 128), F32)]
        + [jax.ShapeDtypeStruct((16, SLOT, 128), F32)] * 2,
        in_specs=[hbm] * 9,
        out_specs=[free] * 3,
        scratch_shapes=[
            flats, flats, flats,
            pltpu.VMEM((16, 128), F32),
            pltpu.VMEM((16, 128), jnp.int32),
            pltpu.SMEM((NREG, NPAR), F32),
            pltpu.VMEM((NPAR, NMODE), jnp.int32),
            pltpu.VMEM((NPAR, NQ), jnp.int32),
            pltpu.VMEM((1, NQ), jnp.int32),
            blocks, blocks, blocks, blocks,
            field, field, field, field, field, field, blocks,
            pair, packed, pair, packed, pair,
            edge, edge,
            pltpu.VMEM((128, 512), F32),
            pltpu.VMEM((256, 128), F32),
            pltpu.VMEM((16, 256), F32),
            pltpu.VMEM((3, 16, NQ), F32),
            pltpu.VMEM((NQ, 128), F32),
            pltpu.VMEM((KP, NQ), F32),
            pltpu.VMEM((NREG * ROWS, 3 * KP), BF16),
            pltpu.VMEM((NQ, 3 * KP), BF16),
            pltpu.VMEM((ROWS, 3 * NQ), BF16),
            pltpu.VMEM((3 * KP, 512), BF16),
            pltpu.VMEM((NREG * ROWS, 512), F32),
            pltpu.VMEM((3 * KP, 3 * 512), BF16),
            pltpu.VMEM((NQ, 512), F32),
            pltpu.VMEM((3 * NQ, 512), BF16),
            pltpu.VMEM((NREG, NQ, 128), F32),
            pltpu.SemaphoreType.DMA((9,)),
            pltpu.SemaphoreType.DMA((5,)),
            pltpu.SemaphoreType.DMA((5,)),
            pltpu.SemaphoreType.DMA((10,)),
            pltpu.SemaphoreType.DMA((10,)),
        ],
        compiler_params=pltpu.CompilerParams(
            collective_id=0, has_side_effects=True, vmem_limit_bytes=36 << 20
        ),
        name="step",
    )(*(
        pltpu.with_memory_space_constraint(x, pltpu.HBM)
        for x in (
            flat(v), flat(i), flat(t), avg.reshape(16, 128), zone.reshape(16, 128), zrr,
            exps.T, choice.T, share.reshape(1, NQ),
        )
    ))
    rel, adv = pl.pallas_call(
        assemble,
        out_shape=[jax.ShapeDtypeStruct((GRP * 16, 128), F32)] * 2,
        in_specs=[free, vmem, vmem],
        out_specs=[free] * 2,
        scratch_shapes=[flats, pltpu.SemaphoreType.DMA((2,))],
        compiler_params=pltpu.CompilerParams(vmem_limit_bytes=16 << 20),
        name="assemble",
    )(*parts)
    shape = (GRP, 1, 2048)
    return rel.reshape(shape), adv.reshape(shape)


def solution(mesh):
    field = P("modes", "space", None)
    cells = P("space", None)
    return jax.shard_map(
        on_device,
        mesh=mesh,
        in_specs=(field, field, field, cells, cells, P(), P(), P(), P()),
        out_specs=(field, field),
        check_vma=False,
    )
```

```python
import functools
import math

import jax
import jax.numpy as jnp
from jax import lax
from jax.experimental import pallas as pl
from jax.experimental.pallas import tpu as pltpu
from jax.sharding import PartitionSpec as P

MESH = pl.DeviceIdType.MESH
F32 = jnp.float32
BF16 = jnp.bfloat16
NODE_A = 1.355626179974266
NODE_B = 2.8569700138728056
NMODE = 220
NPAR = 9
NQ = 512
NREG = 4
GRP = 55
SLOT = 56
ROWS = 4 * SLOT
KP = 256
MIX = 0.8 / 6.0
COLUMNS = 32
FAR = 100.0


def split(x):
    hi = x.astype(BF16)
    return hi, (x - hi.astype(F32)).astype(BF16)


def kernel(
    v_hbm, i_hbm, t_hbm, avg_hbm, zone_hbm, zrr_hbm, e_hbm, n_hbm, share_hbm,
    rel_out, ao, tfix_out,
    v_ref, i_ref, t_ref, avg_ref, zone_ref, zrr_ref, e_ref, n_ref, share_ref,
    sv, su, st, tfix, vc, uc, tc, rel, adv, rough, ro, hxv, hyv, hxr, hyr, hxt, pkv, pkr,
    tmp, ecol, erow, hrow, ncol, basis_t, acat, bcat, wcat, rcat, pmix, gcat, jsum, jcat, lift,
    in_sem, a_send, a_recv, h_send, h_recv,
):
    s = lax.axis_index("space")
    m = lax.axis_index("modes")
    k = s // 4
    p = s % 4
    z = (p // 2) * 4 + m
    c = p % 2
    b = z * 2 + c

    def at_chip(col, zz, cc):
        return (col * 4 + (zz // 4) * 2 + cc, zz % 4)

    def at_block(col, bb):
        return at_chip(col, bb // 2, bb % 2)

    k_next, k_prev = (k + 1) % COLUMNS, (k + COLUMNS - 1) % COLUMNS
    b_next, b_prev = (b + 1) % 16, (b + 15) % 16
    hops = [(d, cc) for d in (4, 3, 5, 2, 6, 1, 7) for cc in (0, 1)]

    loads = [
        pltpu.make_async_copy(src, dst, in_sem.at[n])
        for n, (src, dst) in enumerate((
            (v_hbm, v_ref), (avg_hbm, avg_ref), (i_hbm, i_ref), (zone_hbm, zone_ref),
            (t_hbm, t_ref), (zrr_hbm, zrr_ref), (e_hbm, e_ref), (n_hbm, n_ref), (share_hbm, share_ref)))
    ]
    loads[0].start()
    loads[1].start()

    for g in range(4):
        tc[:, g * SLOT + GRP : (g + 1) * SLOT] = jnp.zeros((4, 1, 128), F32)

    bar = pltpu.get_barrier_semaphore()

    def greet(dev):
        pl.semaphore_signal(bar, inc=1, device_id=dev, device_id_type=MESH)

    for d, cc in hops:
        greet(at_chip(k, (z + d) % 8, cc))
    greet(at_chip(k, z, 1 - c))
    greet(at_chip(k_next, z, c))
    greet(at_chip(k_prev, z, c))
    for load in loads[2:]:
        load.start()

    def remote(src, dst, ssem, rsem, dev):
        cp = pltpu.make_async_remote_copy(
            src, dst, ssem, rsem, device_id=dev, device_id_type=MESH
        )
        cp.start()

    def slot(ref, pp, mm, size=SLOT):
        return ref.at[pp, pl.ds(pl.multiple_of(mm * SLOT, 8), size)]

    first = [hop for hop in hops if hop[0] in (3, 5)]
    second = [hop for hop in hops if hop[0] in (4, 2, 6)]
    third = [hop for hop in hops if hop[0] in (1, 7)]

    def send_to(f, src, place, some):
        for d, cc in some:
            z2 = (z + d) % 8
            remote(src.at[z2 * 2 + cc, pl.ds(0, place.shape[0])], place, a_send.at[f], a_recv.at[f], at_chip(k, z2, cc))

    def send_rest(f, src, place):
        size = pl.ds(0, place.shape[0])
        remote(src.at[z * 2 + 1 - c, size], place, a_send.at[f], a_recv.at[f],
               at_chip(k, z, 1 - c))
        pltpu.make_async_copy(src.at[b, size], place, a_recv.at[f]).start()

    def send_out(f, src, dst, outer):
        place = dst.at[b, pl.ds(0, GRP)]
        for d in (4, 3, 5, 2, 6, 1, 7, 0):
            z2 = (z + d) % 8
            zh = z2 // 4
            cc = zh if outer else 1 - zh
            if d:
                remote(slot(src, zh * 2 + cc, z2 % 4, GRP), place, a_send.at[f], a_recv.at[f],
                       at_chip(k, z2, cc))
                continue
            block = slot(src, zh * 2 + cc, m, GRP)

            @pl.when(cc == c)
            def _():
                pltpu.make_async_copy(block, place, a_recv.at[f]).start()

            @pl.when(cc != c)
            def _():
                remote(block, place, a_send.at[f], a_recv.at[f], at_chip(k, z, 1 - c))

    def await_all(f, buf):
        if f >= 2:
            buf = buf.at[:, pl.ds(0, 4 * GRP)] if f == 2 else buf.at[:, pl.ds(0, GRP)]
        pltpu.make_async_copy(buf, buf, a_recv.at[f]).wait()

    def await_sent(f, buf):
        part = buf.at[pl.ds(0, 15), pl.ds(0, SLOT if f < 2 else GRP)]
        pltpu.make_async_copy(part, part, a_send.at[f]).wait()

    def halo(j, src, dst, dev):
        remote(src, dst, h_send.at[j], h_recv.at[j], dev)

    def await_halo(j, ref):
        pltpu.make_async_copy(ref, ref, h_recv.at[j]).wait()

    def await_halo_sent(j, ref):
        pltpu.make_async_copy(ref, ref, h_send.at[j]).wait()

    lane1 = lax.broadcasted_iota(jnp.int32, (1, 128), 1)
    low8 = lane1 < 8
    high8 = lane1 >= 120
    octet = lane1 // 8

    loads[0].wait()
    loads[1].wait()
    for bb in range(16):
        sv[bb, 0:GRP] = v_ref[pl.ds(bb, GRP, stride=16), :]
        sv[bb, GRP:SLOT] = avg_ref[bb : bb + 1, :]
    pl.semaphore_wait(bar, 17)
    send_to(0, sv, slot(vc, p, m), hops)
    send_rest(0, sv, slot(vc, p, m))

    loads[4].wait()
    for bb in range(16):
        st[bb, 0:GRP] = t_ref[pl.ds(bb, GRP, stride=16), :]
        st[bb, GRP:SLOT] = jnp.zeros((1, 128), F32)
    send_to(2, st, slot(tc, p, m, GRP), first)
    loads[2].wait()
    loads[3].wait()
    for bb in range(16):
        gain = MIX / avg_ref[bb : bb + 1, :]
        su[bb, 0:GRP] = sv[bb, 0:GRP] + i_ref[pl.ds(bb, GRP, stride=16), :] * gain
        su[bb, GRP:SLOT] = zone_ref[bb : bb + 1, :].astype(F32)
    for load in loads[5:]:
        load.wait()

    tmp[...] = jnp.zeros((128, 512), F32)
    tmp[0:NPAR, 0:NMODE] = e_ref[...].astype(F32)
    raw = tmp[0:16, 0:256]
    lane = lax.broadcasted_iota(jnp.int32, (16, 256), 1)
    spaced = jnp.full((16, 256), FAR, F32)
    for g in range(4):
        here = (lane >= SLOT * g) & (lane < SLOT * g + GRP)
        spaced = jnp.where(here, raw if g == 0 else pltpu.roll(raw, g, 1), spaced)
    erow[...] = spaced
    tmp[0:16, 0:256] = spaced
    ecol[...] = jnp.transpose(tmp[:, 0:256])

    choice = n_ref[...]
    node = jnp.where(
        choice == 1, NODE_A,
        jnp.where(choice == 2, -NODE_A,
                  jnp.where(choice == 3, NODE_B, jnp.where(choice == 4, -NODE_B, 0.0))))
    tmp[...] = jnp.zeros((128, 512), F32)
    tmp[0:NPAR, :] = node
    hrow[0, 0:NPAR] = node
    hrow[1, 0:NPAR] = (node * node - 1.0) * (1.0 / math.sqrt(2.0))
    hrow[2, 0:NPAR] = (node * node * node - 3.0 * node) * (1.0 / math.sqrt(6.0))
    ncol[...] = jnp.transpose(tmp[...])

    def basis_rows(i, _):
        rows = pl.ds(pl.multiple_of(i * 8, 8), 8)
        acc = jnp.ones((8, NQ), F32)
        for par in range(NPAR):
            e = ecol[rows, par : par + 1]
            f = jnp.where(e == 1.0, hrow[0, par : par + 1, :], 1.0)
            f = jnp.where(e == 2.0, hrow[1, par : par + 1, :], f)
            f = jnp.where(e == 3.0, hrow[2, par : par + 1, :], f)
            acc = acc * f
        basis_t[rows, :] = jnp.where(ecol[rows, 0:1] < 50.0, acc, 0.0)
        return 0

    lax.fori_loop(0, KP // 8, basis_rows, 0)
    hi, lo = split(jnp.transpose(basis_t[...]))
    bcat[:, 0:KP] = hi
    bcat[:, KP : 2 * KP] = hi
    bcat[:, 2 * KP : 3 * KP] = lo
    weight = share_ref[...].astype(F32) * (1.0 / (512.0 * NQ * NMODE))
    hi, lo = split(basis_t[0:ROWS, :] * weight)
    wcat[:, 0:NQ] = hi
    wcat[:, NQ : 2 * NQ] = hi
    wcat[:, 2 * NQ : 3 * NQ] = lo

    def coupling_rows(i, _):
        rows = pl.ds(pl.multiple_of(i * 16, 16), 16)
        apart = jnp.zeros((16, KP), F32)
        acc = [jnp.zeros((16, KP), F32) for _ in range(NREG)]
        for par in range(NPAR):
            ei = ecol[rows, par : par + 1]
            ej = erow[par : par + 1, :]
            diff = jnp.abs(ei - ej)
            larger = jnp.maximum(ei, ej)
            root = jnp.where(larger == 1.0, 1.0,
                             jnp.where(larger == 2.0, math.sqrt(2.0), math.sqrt(3.0)))
            apart = apart + diff
            link = diff * root
            for r in range(NREG):
                acc[r] = acc[r] + zrr_ref[r, par] * link
        for r in range(NREG):
            hi, lo = split(jnp.where(apart == 1.0, acc[r], 0.0))
            out = pl.ds(pl.multiple_of(r * ROWS + i * 16, 16), 16)
            acat[out, 0:KP] = hi
            acat[out, KP : 2 * KP] = hi
            acat[out, 2 * KP : 3 * KP] = lo
        return 0

    lax.fori_loop(0, ROWS // 16, coupling_rows, 0)

    for part in range(3):
        gcat[part * KP + ROWS : (part + 1) * KP, :] = jnp.zeros((KP - ROWS, 3 * 512), BF16)
        rcat[part * KP + ROWS : (part + 1) * KP, :] = jnp.zeros((KP - ROWS, 512), BF16)

    depth = lane1 % 8
    z_has_next = depth < 7
    z_has_prev = depth > 0
    k_low = (k > 0).astype(F32)
    k_high = (k < COLUMNS - 1).astype(F32)
    b_low = (b > 0).astype(F32)
    b_high = (b < 15).astype(F32)

    chunk = 32
    chunks = ROWS // chunk

    def chunk_of(i):
        return pl.ds(pl.multiple_of(i * chunk, chunk), chunk)

    def y_pair(x, edges):
        after, before = edges
        y_next = jnp.where(high8, after, pltpu.roll(x, 120, 1))
        y_prev = jnp.where(low8, before, pltpu.roll(x, 8, 1))
        return y_next, y_prev

    def z_pair(x):
        z_next = jnp.where(z_has_next, pltpu.roll(x, 127, 1), 0.0)
        z_prev = jnp.where(z_has_prev, pltpu.roll(x, 1, 1), 0.0)
        return z_next, z_prev

    def x_pair(field, hx, q, rows):
        x_next = field[q + 1, rows, :] if q < 3 else hx[1, rows, :] * k_high
        x_prev = field[q - 1, rows, :] if q > 0 else hx[0, rows, :] * k_low
        return x_next, x_prev

    def exchange_x(j, field, hx):
        halo(j, field.at[3], hx.at[0], at_chip(k_next, z, c))
        halo(j + 1, field.at[0], hx.at[1], at_chip(k_prev, z, c))

    def exchange_y(j, pk, hy):
        halo(j, pk.at[0], hy.at[0], at_block(k, b_next))
        halo(j + 1, pk.at[1], hy.at[1], at_block(k, b_prev))

    await_all(0, vc)
    exchange_x(0, vc, hxv)

    def turn(x, shift):
        return pltpu.roll(x, shift % 128, 1) if shift % 128 else x

    def pack(src, dst):
        for i in range(chunks):
            last = jnp.zeros((8, 128), F32)
            start = jnp.zeros((8, 128), F32)
            for j in range(4):
                for q in range(4):
                    x = src[q, 32 * i + 8 * j : 32 * i + 8 * j + 8, :]
                    here = octet == 4 * j + q
                    last = jnp.where(here, turn(x, 32 * j + 8 * q + 8), last)
                    start = jnp.where(here, turn(x, 32 * j + 8 * q), start)
            dst[0, 8 * i : 8 * i + 8, :] = last
            dst[1, 8 * i : 8 * i + 8, :] = start

    def edges_of(hy, i):
        tile = pl.ds(pl.multiple_of(i * 8, 8), 8)
        below = hy[0, tile, :] * b_low
        above = hy[1, tile, :] * b_high
        return [
            (jnp.concatenate([turn(above, 120 - 32 * j - 8 * q) for j in range(4)], axis=0),
             jnp.concatenate([turn(below, -32 * j - 8 * q) for j in range(4)], axis=0))
            for q in range(4)
        ]

    pack(vc, pkv)
    exchange_y(2, pkv, hyv)
    send_to(1, su, slot(uc, p, m), hops)
    send_rest(1, su, slot(uc, p, m))
    send_to(2, st, slot(tc, p, m, GRP), second)
    send_rest(2, st, slot(tc, p, m, GRP))

    def lift_rows(i, _):
        rows = pl.ds(pl.multiple_of(i * 8, 8), 8)
        acc = [jnp.ones((8, 128), F32) for _ in range(NREG)]
        for par in range(NPAR):
            nd = jnp.broadcast_to(ncol[rows, par : par + 1], (8, 128))
            for r in range(NREG):
                acc[r] = acc[r] + zrr_ref[r, par] * nd
        for r in range(NREG):
            lift[r, rows, :] = acc[r]
        return 0

    lax.fori_loop(0, NQ // 8, lift_rows, 0)

    await_halo(0, hxv.at[0])
    await_halo(1, hxv.at[1])
    await_halo(2, hyv.at[0])
    await_halo(3, hyv.at[1])

    def rough_rows(i, _):
        rows = chunk_of(i)
        edges = edges_of(hyv, i)
        for q in range(4):
            x = vc[q, rows, :]
            y_next, y_prev = y_pair(x, edges[q])
            z_next, z_prev = z_pair(x)
            x_next, x_prev = x_pair(vc, hxv, q, rows)
            value = 6.0 * x - x_next - x_prev - z_next - z_prev - y_next - y_prev
            rough[q, rows, :] = value
            hi, lo = split(value)
            base = i * chunk
            cols = slice(128 * q, 128 * q + 128)
            rcat[pl.ds(pl.multiple_of(base, chunk), chunk), cols] = hi
            rcat[pl.ds(pl.multiple_of(base + KP, chunk), chunk), cols] = lo
            rcat[pl.ds(pl.multiple_of(base + 2 * KP, chunk), chunk), cols] = hi
        return 0

    lax.fori_loop(0, chunks, rough_rows, 0)

    def mix_region(r, _):
        rows = pl.ds(pl.multiple_of(r * ROWS, 32), ROWS)
        pmix[rows, :] = jnp.dot(acat[rows, :], rcat[...], preferred_element_type=F32)
        return 0

    lax.fori_loop(0, NREG, mix_region, 0)

    await_all(1, uc)
    zones = [uc[q, GRP : GRP + 1, :] for q in range(4)]
    avgs = [vc[q, GRP : GRP + 1, :] for q in range(4)]

    def relax_rows(i, _):
        rows = chunk_of(i)
        for q in range(4):
            cols = slice(128 * q, 128 * q + 128)
            part = [
                pmix[pl.ds(pl.multiple_of(r * ROWS + i * chunk, chunk), chunk), cols]
                for r in range(NREG)
            ]
            mixed = part[3]
            for r in range(3):
                mixed = jnp.where(zones[q] == float(r), part[r], mixed)
            rel[q, rows, :] = uc[q, rows, :] - MIX * (rough[q, rows, :] + mixed)
        return 0

    lax.fori_loop(0, chunks, relax_rows, 0)
    exchange_x(4, rel, hxr)
    pack(rel, pkr)
    exchange_y(6, pkr, hyr)
    send_to(2, st, slot(tc, p, m, GRP), third)
    send_out(3, rel, ro, False)
    send_out(3, rel, ro, True)

    def put_grad(i, col, value):
        hi, lo = split(value)
        base = i * chunk
        cols = slice(col, col + 128)
        gcat[pl.ds(pl.multiple_of(base, chunk), chunk), cols] = hi
        gcat[pl.ds(pl.multiple_of(base + KP, chunk), chunk), cols] = lo
        gcat[pl.ds(pl.multiple_of(base + 2 * KP, chunk), chunk), cols] = hi

    def grad_z(i, _):
        rows = chunk_of(i)
        for q in range(4):
            z_next, z_prev = z_pair(rel[q, rows, :])
            put_grad(i, 1024 + 128 * q, z_next - z_prev)
        return 0

    lax.fori_loop(0, chunks, grad_z, 0)

    def at_points(col, half):
        cols = pl.ds(pl.multiple_of(col + half * 256, 256), 256)
        return jnp.dot(bcat[...], gcat[:, cols], preferred_element_type=F32)

    def half_cols(half):
        return pl.ds(pl.multiple_of(half * 256, 256), 256)

    def points_z(half, _):
        g = at_points(1024, half)
        jsum[:, half_cols(half)] = g * g
        return 0

    lax.fori_loop(0, 2, points_z, 0)

    await_halo(4, hxr.at[0])
    await_halo(5, hxr.at[1])
    await_halo(6, hyr.at[0])
    await_halo(7, hyr.at[1])

    def grad_xy(i, _):
        rows = chunk_of(i)
        edges = edges_of(hyr, i)
        for q in range(4):
            y_next, y_prev = y_pair(rel[q, rows, :], edges[q])
            x_next, x_prev = x_pair(rel, hxr, q, rows)
            put_grad(i, 128 * q, x_next - x_prev)
            put_grad(i, 512 + 128 * q, y_next - y_prev)
        return 0

    lax.fori_loop(0, chunks, grad_xy, 0)

    def points_xy(half, _):
        cols = half_cols(half)
        g = at_points(0, half)
        jsum[:, cols] = jsum[:, cols] + g * g
        g = at_points(512, half)
        jsum[:, cols] = jsum[:, cols] + g * g
        return 0

    lax.fori_loop(0, 2, points_xy, 0)

    await_all(2, tc)
    exchange_x(8, tc, hxt)

    def joule_rows(i, _):
        rows = chunk_of(i)
        for q in range(4):
            gain = lift[3, rows, :]
            for r in range(3):
                gain = jnp.where(zones[q] == float(r), lift[r, rows, :], gain)
            cols = slice(128 * q, 128 * q + 128)
            hi, lo = split(jsum[rows, cols] * gain)
            base = i * chunk
            jcat[pl.ds(pl.multiple_of(base, chunk), chunk), cols] = hi
            jcat[pl.ds(pl.multiple_of(base + NQ, chunk), chunk), cols] = lo
            jcat[pl.ds(pl.multiple_of(base + 2 * NQ, chunk), chunk), cols] = hi
        return 0

    lax.fori_loop(0, NQ // chunk, joule_rows, 0)

    def heat_half(half, _):
        cols = half_cols(half)
        pmix[0:ROWS, cols] = jnp.dot(wcat[...], jcat[:, cols], preferred_element_type=F32)
        return 0

    lax.fori_loop(0, 2, heat_half, 0)
    def adv_rows(outer):
        def body(i, _):
            rows = chunk_of(i)
            for q in (0, 3) if outer else (1, 2):
                t_next, t_prev = x_pair(tc, hxt, q, rows)
                scale = avgs[q] * 0.025
                adv[q, rows, :] = (
                    pmix[rows, 128 * q : 128 * q + 128] * scale + 0.15 * (t_next + t_prev)
                )
            return 0

        lax.fori_loop(0, chunks, body, 0)

    adv_rows(False)
    send_out(4, adv, ao, False)
    await_halo(8, hxt.at[0])
    await_halo(9, hxt.at[1])
    adv_rows(True)
    send_out(4, adv, ao, True)

    def tfix_block(bb, _):
        cur = st[bb]
        before = st[jnp.maximum(bb - 1, 0)] * (bb > 0).astype(F32)
        after = st[jnp.minimum(bb + 1, 15)] * (bb < 15).astype(F32)
        y_next = jnp.where(high8, pltpu.roll(after, 120, 1), pltpu.roll(cur, 120, 1))
        y_prev = jnp.where(low8, pltpu.roll(before, 8, 1), pltpu.roll(cur, 8, 1))
        z_next = jnp.where(z_has_next, pltpu.roll(cur, 127, 1), 0.0)
        z_prev = jnp.where(z_has_prev, pltpu.roll(cur, 1, 1), 0.0)
        tfix[bb] = cur - 0.15 * (6.0 * cur - y_next - y_prev - z_next - z_prev)
        return 0

    lax.fori_loop(0, 16, tfix_block, 0)

    local = pltpu.make_async_copy(tfix, tfix_out, in_sem.at[0])
    local.start()
    await_all(3, ro)
    for bb in range(16):
        v_ref[pl.ds(bb, GRP, stride=16), :] = ro[bb, 0:GRP]
    final = pltpu.make_async_copy(v_ref, rel_out, in_sem.at[1])
    final.start()
    for f in range(4):
        await_sent(f, sv)
    for j in (0, 1, 4, 5, 8, 9):
        await_halo_sent(j, hxv.at[0])
    for j in (2, 3, 6, 7):
        await_halo_sent(j, pkr.at[0])
    local.wait()
    final.wait()
    await_sent(4, sv)
    await_all(4, ao)


def assemble(rel, ao, tfix, rel_out, adv_out, adv, sem):
    first = pltpu.make_async_copy(rel, rel_out, sem.at[0])
    first.start()
    for bb in range(16):
        adv[pl.ds(bb, GRP, stride=16), :] = ao[bb, 0:GRP] + tfix[bb, 0:GRP]
    second = pltpu.make_async_copy(adv, adv_out, sem.at[1])
    second.start()
    first.wait()
    second.wait()


def on_device(v, i, t, avg, zone, zrr, exps, choice, share):
    flat = lambda x: x.reshape(GRP * 16, 128)
    vmem = pl.BlockSpec(memory_space=pltpu.VMEM)
    hbm = pl.BlockSpec(memory_space=pltpu.HBM)
    free = pl.BlockSpec(memory_space=pl.ANY)
    field = pltpu.VMEM((4, ROWS, 128), F32)
    blocks = pltpu.VMEM((16, SLOT, 128), F32)
    pair = pltpu.VMEM((2, ROWS, 128), F32)
    flats = pltpu.VMEM((GRP * 16, 128), F32)
    packed = pltpu.VMEM((2, ROWS // 4, 128), F32)
    parts = pl.pallas_call(
        kernel,
        out_shape=[jax.ShapeDtypeStruct((GRP * 16, 128), F32)]
        + [jax.ShapeDtypeStruct((16, SLOT, 128), F32)] * 2,
        in_specs=[hbm] * 9,
        out_specs=[free] * 3,
        scratch_shapes=[
            flats, flats, flats,
            pltpu.VMEM((16, 128), F32),
            pltpu.VMEM((16, 128), jnp.int32),
            pltpu.SMEM((NREG, NPAR), F32),
            pltpu.VMEM((NPAR, NMODE), jnp.int32),
            pltpu.VMEM((NPAR, NQ), jnp.int32),
            pltpu.VMEM((1, NQ), jnp.int32),
            blocks, blocks, blocks, blocks,
            field, field, field, field, field, field, blocks,
            pair, packed, pair, packed, pair,
            packed, packed,
            pltpu.VMEM((128, 512), F32),
            pltpu.VMEM((256, 128), F32),
            pltpu.VMEM((16, 256), F32),
            pltpu.VMEM((3, 16, NQ), F32),
            pltpu.VMEM((NQ, 128), F32),
            pltpu.VMEM((KP, NQ), F32),
            pltpu.VMEM((NREG * ROWS, 3 * KP), BF16),
            pltpu.VMEM((NQ, 3 * KP), BF16),
            pltpu.VMEM((ROWS, 3 * NQ), BF16),
            pltpu.VMEM((3 * KP, 512), BF16),
            pltpu.VMEM((NREG * ROWS, 512), F32),
            pltpu.VMEM((3 * KP, 3 * 512), BF16),
            pltpu.VMEM((NQ, 512), F32),
            pltpu.VMEM((3 * NQ, 512), BF16),
            pltpu.VMEM((NREG, NQ, 128), F32),
            pltpu.SemaphoreType.DMA((9,)),
            pltpu.SemaphoreType.DMA((5,)),
            pltpu.SemaphoreType.DMA((5,)),
            pltpu.SemaphoreType.DMA((10,)),
            pltpu.SemaphoreType.DMA((10,)),
        ],
        compiler_params=pltpu.CompilerParams(
            collective_id=0, has_side_effects=True, vmem_limit_bytes=36 << 20
        ),
        name="step",
    )(*(
        pltpu.with_memory_space_constraint(x, pltpu.HBM)
        for x in (
            flat(v), flat(i), flat(t), avg.reshape(16, 128), zone.reshape(16, 128), zrr,
            exps.T, choice.T, share.reshape(1, NQ),
        )
    ))
    rel, adv = pl.pallas_call(
        assemble,
        out_shape=[jax.ShapeDtypeStruct((GRP * 16, 128), F32)] * 2,
        in_specs=[free, vmem, vmem],
        out_specs=[free] * 2,
        scratch_shapes=[flats, pltpu.SemaphoreType.DMA((2,))],
        compiler_params=pltpu.CompilerParams(vmem_limit_bytes=16 << 20),
        name="assemble",
    )(*parts)
    shape = (GRP, 1, 2048)
    return rel.reshape(shape), adv.reshape(shape)


def solution(mesh):
    field = P("modes", "space", None)
    cells = P("space", None)
    return jax.shard_map(
        on_device,
        mesh=mesh,
        in_specs=(field, field, field, cells, cells, P(), P(), P(), P()),
        out_specs=(field, field),
        check_vma=False,
    )
```

```python
import functools
import math

import jax
import jax.numpy as jnp
from jax import lax
from jax.experimental import pallas as pl
from jax.experimental.pallas import tpu as pltpu
from jax.sharding import PartitionSpec as P

MESH = pl.DeviceIdType.MESH
F32 = jnp.float32
BF16 = jnp.bfloat16
NODE_A = 1.355626179974266
NODE_B = 2.8569700138728056
NMODE = 220
NPAR = 9
NQ = 512
NREG = 4
GRP = 55
SLOT = 56
ROWS = 4 * SLOT
KP = 256
MIX = 0.8 / 6.0
COLUMNS = 32
FAR = 100.0


def split(x):
    hi = x.astype(BF16)
    return hi, (x - hi.astype(F32)).astype(BF16)


def kernel(
    v_hbm, i_hbm, t_hbm, avg_hbm, zone_hbm, zrr_hbm, e_hbm, n_hbm, share_hbm,
    rel_out, ao, tfix_out,
    v_ref, i_ref, t_ref, avg_ref, zone_ref, zrr_ref, e_ref, n_ref, share_ref,
    sv, su, st, tfix, vc, uc, tc, rel, adv, rough, ro, hxv, hyv, hxr, hyr, hxt, pkv, pkr,
    tmp, ecol, erow, hrow, ncol, basis_t, acat, bcat, wcat, rcat, pmix, gcat, jsum, jcat, lift,
    in_sem, a_send, a_recv, h_send, h_recv,
):
    s = lax.axis_index("space")
    m = lax.axis_index("modes")
    k = s // 4
    p = s % 4
    z = (p // 2) * 4 + m
    c = p % 2
    b = z * 2 + c

    def at_chip(col, zz, cc):
        return (col * 4 + (zz // 4) * 2 + cc, zz % 4)

    def at_block(col, bb):
        return at_chip(col, bb // 2, bb % 2)

    k_next, k_prev = (k + 1) % COLUMNS, (k + COLUMNS - 1) % COLUMNS
    b_next, b_prev = (b + 1) % 16, (b + 15) % 16
    hops = [(d, cc) for d in (4, 3, 5, 2, 6, 1, 7) for cc in (0, 1)]

    loads = [
        pltpu.make_async_copy(src, dst, in_sem.at[n])
        for n, (src, dst) in enumerate((
            (v_hbm, v_ref), (avg_hbm, avg_ref), (i_hbm, i_ref), (zone_hbm, zone_ref),
            (t_hbm, t_ref), (zrr_hbm, zrr_ref), (e_hbm, e_ref), (n_hbm, n_ref), (share_hbm, share_ref)))
    ]
    loads[0].start()
    loads[1].start()

    for g in range(4):
        tc[:, g * SLOT + GRP : (g + 1) * SLOT] = jnp.zeros((4, 1, 128), F32)

    bar = pltpu.get_barrier_semaphore()

    def greet(dev):
        pl.semaphore_signal(bar, inc=1, device_id=dev, device_id_type=MESH)

    for d, cc in hops:
        greet(at_chip(k, (z + d) % 8, cc))
    greet(at_chip(k, z, 1 - c))
    greet(at_chip(k_next, z, c))
    greet(at_chip(k_prev, z, c))
    for load in loads[2:]:
        load.start()

    def remote(src, dst, ssem, rsem, dev):
        cp = pltpu.make_async_remote_copy(
            src, dst, ssem, rsem, device_id=dev, device_id_type=MESH
        )
        cp.start()

    def slot(ref, pp, mm, size=SLOT):
        return ref.at[pp, pl.ds(pl.multiple_of(mm * SLOT, 8), size)]

    first = [hop for hop in hops if hop[0] in (3, 5)]
    rest = [hop for hop in hops if hop[0] not in (3, 5)]
    early = [hop for hop in hops if hop[0] in (3, 5, 1, 7)]
    late = [hop for hop in hops if hop[0] in (4, 2, 6)]

    def send_to(f, src, place, some):
        for d, cc in some:
            z2 = (z + d) % 8
            remote(src.at[z2 * 2 + cc, pl.ds(0, place.shape[0])], place, a_send.at[f], a_recv.at[f], at_chip(k, z2, cc))

    def send_rest(f, src, place):
        size = pl.ds(0, place.shape[0])
        remote(src.at[z * 2 + 1 - c, size], place, a_send.at[f], a_recv.at[f],
               at_chip(k, z, 1 - c))
        pltpu.make_async_copy(src.at[b, size], place, a_recv.at[f]).start()

    def send_out(f, src, dst, outer):
        place = dst.at[b, pl.ds(0, GRP)]
        for d in (4, 3, 5, 2, 6, 1, 7, 0):
            z2 = (z + d) % 8
            zh = z2 // 4
            cc = zh if outer else 1 - zh
            if d:
                remote(slot(src, zh * 2 + cc, z2 % 4, GRP), place, a_send.at[f], a_recv.at[f],
                       at_chip(k, z2, cc))
                continue
            block = slot(src, zh * 2 + cc, m, GRP)

            @pl.when(cc == c)
            def _():
                pltpu.make_async_copy(block, place, a_recv.at[f]).start()

            @pl.when(cc != c)
            def _():
                remote(block, place, a_send.at[f], a_recv.at[f], at_chip(k, z, 1 - c))

    def await_all(f, buf):
        if f >= 2:
            buf = buf.at[:, pl.ds(0, 4 * GRP)] if f == 2 else buf.at[:, pl.ds(0, GRP)]
        pltpu.make_async_copy(buf, buf, a_recv.at[f]).wait()

    def await_sent(f, buf):
        part = buf.at[pl.ds(0, 15), pl.ds(0, SLOT if f < 2 else GRP)]
        pltpu.make_async_copy(part, part, a_send.at[f]).wait()

    def halo(j, src, dst, dev):
        remote(src, dst, h_send.at[j], h_recv.at[j], dev)

    def await_halo(j, ref):
        pltpu.make_async_copy(ref, ref, h_recv.at[j]).wait()

    def await_halo_sent(j, ref):
        pltpu.make_async_copy(ref, ref, h_send.at[j]).wait()

    lane1 = lax.broadcasted_iota(jnp.int32, (1, 128), 1)
    low8 = lane1 < 8
    high8 = lane1 >= 120
    octet = lane1 // 8

    loads[0].wait()
    loads[1].wait()
    for bb in range(16):
        sv[bb, 0:GRP] = v_ref[pl.ds(bb, GRP, stride=16), :]
        sv[bb, GRP:SLOT] = avg_ref[bb : bb + 1, :]
    pl.semaphore_wait(bar, 17)
    send_to(0, sv, slot(vc, p, m), hops)
    send_rest(0, sv, slot(vc, p, m))

    loads[2].wait()
    loads[3].wait()
    for bb in range(16):
        gain = MIX / avg_ref[bb : bb + 1, :]
        su[bb, 0:GRP] = sv[bb, 0:GRP] + i_ref[pl.ds(bb, GRP, stride=16), :] * gain
        su[bb, GRP:SLOT] = zone_ref[bb : bb + 1, :].astype(F32)
    send_to(1, su, slot(uc, p, m), first)
    loads[4].wait()
    for bb in range(16):
        st[bb, 0:GRP] = t_ref[pl.ds(bb, GRP, stride=16), :]
        st[bb, GRP:SLOT] = jnp.zeros((1, 128), F32)
    for load in loads[5:]:
        load.wait()

    tmp[...] = jnp.zeros((128, 512), F32)
    tmp[0:NPAR, 0:NMODE] = e_ref[...].astype(F32)
    raw = tmp[0:16, 0:256]
    lane = lax.broadcasted_iota(jnp.int32, (16, 256), 1)
    spaced = jnp.full((16, 256), FAR, F32)
    for g in range(4):
        here = (lane >= SLOT * g) & (lane < SLOT * g + GRP)
        spaced = jnp.where(here, raw if g == 0 else pltpu.roll(raw, g, 1), spaced)
    erow[...] = spaced
    tmp[0:16, 0:256] = spaced
    ecol[...] = jnp.transpose(tmp[:, 0:256])

    choice = n_ref[...]
    node = jnp.where(
        choice == 1, NODE_A,
        jnp.where(choice == 2, -NODE_A,
                  jnp.where(choice == 3, NODE_B, jnp.where(choice == 4, -NODE_B, 0.0))))
    tmp[...] = jnp.zeros((128, 512), F32)
    tmp[0:NPAR, :] = node
    hrow[0, 0:NPAR] = node
    hrow[1, 0:NPAR] = (node * node - 1.0) * (1.0 / math.sqrt(2.0))
    hrow[2, 0:NPAR] = (node * node * node - 3.0 * node) * (1.0 / math.sqrt(6.0))
    ncol[...] = jnp.transpose(tmp[...])

    def basis_rows(i, _):
        rows = pl.ds(pl.multiple_of(i * 8, 8), 8)
        acc = jnp.ones((8, NQ), F32)
        for par in range(NPAR):
            e = ecol[rows, par : par + 1]
            f = jnp.where(e == 1.0, hrow[0, par : par + 1, :], 1.0)
            f = jnp.where(e == 2.0, hrow[1, par : par + 1, :], f)
            f = jnp.where(e == 3.0, hrow[2, par : par + 1, :], f)
            acc = acc * f
        basis_t[rows, :] = jnp.where(ecol[rows, 0:1] < 50.0, acc, 0.0)
        return 0

    lax.fori_loop(0, KP // 8, basis_rows, 0)
    hi, lo = split(jnp.transpose(basis_t[...]))
    bcat[:, 0:KP] = hi
    bcat[:, KP : 2 * KP] = hi
    bcat[:, 2 * KP : 3 * KP] = lo
    weight = share_ref[...].astype(F32) * (1.0 / (512.0 * NQ * NMODE))
    hi, lo = split(basis_t[0:ROWS, :] * weight)
    wcat[:, 0:NQ] = hi
    wcat[:, NQ : 2 * NQ] = hi
    wcat[:, 2 * NQ : 3 * NQ] = lo

    def coupling_rows(i, _):
        rows = pl.ds(pl.multiple_of(i * 16, 16), 16)
        apart = jnp.zeros((16, KP), F32)
        acc = [jnp.zeros((16, KP), F32) for _ in range(NREG)]
        for par in range(NPAR):
            ei = ecol[rows, par : par + 1]
            ej = erow[par : par + 1, :]
            diff = jnp.abs(ei - ej)
            larger = jnp.maximum(ei, ej)
            root = jnp.where(larger == 1.0, 1.0,
                             jnp.where(larger == 2.0, math.sqrt(2.0), math.sqrt(3.0)))
            apart = apart + diff
            link = diff * root
            for r in range(NREG):
                acc[r] = acc[r] + zrr_ref[r, par] * link
        for r in range(NREG):
            hi, lo = split(jnp.where(apart == 1.0, acc[r], 0.0))
            out = pl.ds(pl.multiple_of(r * ROWS + i * 16, 16), 16)
            acat[out, 0:KP] = hi
            acat[out, KP : 2 * KP] = hi
            acat[out, 2 * KP : 3 * KP] = lo
        return 0

    lax.fori_loop(0, ROWS // 16, coupling_rows, 0)

    for part in range(3):
        gcat[part * KP + ROWS : (part + 1) * KP, :] = jnp.zeros((KP - ROWS, 3 * 512), BF16)
        rcat[part * KP + ROWS : (part + 1) * KP, :] = jnp.zeros((KP - ROWS, 512), BF16)

    depth = lane1 % 8
    z_has_next = depth < 7
    z_has_prev = depth > 0
    k_low = (k > 0).astype(F32)
    k_high = (k < COLUMNS - 1).astype(F32)
    b_low = (b > 0).astype(F32)
    b_high = (b < 15).astype(F32)

    chunk = 32
    chunks = ROWS // chunk

    def chunk_of(i):
        return pl.ds(pl.multiple_of(i * chunk, chunk), chunk)

    def y_pair(x, edges):
        after, before = edges
        y_next = jnp.where(high8, after, pltpu.roll(x, 120, 1))
        y_prev = jnp.where(low8, before, pltpu.roll(x, 8, 1))
        return y_next, y_prev

    def z_pair(x):
        z_next = jnp.where(z_has_next, pltpu.roll(x, 127, 1), 0.0)
        z_prev = jnp.where(z_has_prev, pltpu.roll(x, 1, 1), 0.0)
        return z_next, z_prev

    def x_pair(field, hx, q, rows):
        x_next = field[q + 1, rows, :] if q < 3 else hx[1, rows, :] * k_high
        x_prev = field[q - 1, rows, :] if q > 0 else hx[0, rows, :] * k_low
        return x_next, x_prev

    def exchange_x(j, field, hx):
        halo(j, field.at[3], hx.at[0], at_chip(k_next, z, c))
        halo(j + 1, field.at[0], hx.at[1], at_chip(k_prev, z, c))

    def exchange_y(j, pk, hy):
        halo(j, pk.at[0], hy.at[0], at_block(k, b_next))
        halo(j + 1, pk.at[1], hy.at[1], at_block(k, b_prev))

    await_all(0, vc)
    exchange_x(0, vc, hxv)

    def turn(x, shift):
        return pltpu.roll(x, shift % 128, 1) if shift % 128 else x

    def pack(src, dst):
        for i in range(chunks):
            last = jnp.zeros((8, 128), F32)
            start = jnp.zeros((8, 128), F32)
            for j in range(4):
                for q in range(4):
                    x = src[q, 32 * i + 8 * j : 32 * i + 8 * j + 8, :]
                    here = octet == 4 * j + q
                    last = jnp.where(here, turn(x, 32 * j + 8 * q + 8), last)
                    start = jnp.where(here, turn(x, 32 * j + 8 * q), start)
            dst[0, 8 * i : 8 * i + 8, :] = last
            dst[1, 8 * i : 8 * i + 8, :] = start

    def edges_of(hy, i):
        tile = pl.ds(pl.multiple_of(i * 8, 8), 8)
        below = hy[0, tile, :] * b_low
        above = hy[1, tile, :] * b_high
        return [
            (jnp.concatenate([turn(above, 120 - 32 * j - 8 * q) for j in range(4)], axis=0),
             jnp.concatenate([turn(below, -32 * j - 8 * q) for j in range(4)], axis=0))
            for q in range(4)
        ]

    pack(vc, pkv)
    exchange_y(2, pkv, hyv)
    send_to(1, su, slot(uc, p, m), rest)
    send_rest(1, su, slot(uc, p, m))
    send_to(2, st, slot(tc, p, m, GRP), early)
    send_rest(2, st, slot(tc, p, m, GRP))

    def lift_rows(i, _):
        rows = pl.ds(pl.multiple_of(i * 8, 8), 8)
        acc = [jnp.ones((8, 128), F32) for _ in range(NREG)]
        for par in range(NPAR):
            nd = jnp.broadcast_to(ncol[rows, par : par + 1], (8, 128))
            for r in range(NREG):
                acc[r] = acc[r] + zrr_ref[r, par] * nd
        for r in range(NREG):
            lift[r, rows, :] = acc[r]
        return 0

    lax.fori_loop(0, NQ // 8, lift_rows, 0)

    await_halo(0, hxv.at[0])
    await_halo(1, hxv.at[1])
    await_halo(2, hyv.at[0])
    await_halo(3, hyv.at[1])

    def rough_rows(i, _):
        rows = chunk_of(i)
        edges = edges_of(hyv, i)
        for q in range(4):
            x = vc[q, rows, :]
            y_next, y_prev = y_pair(x, edges[q])
            z_next, z_prev = z_pair(x)
            x_next, x_prev = x_pair(vc, hxv, q, rows)
            value = 6.0 * x - x_next - x_prev - z_next - z_prev - y_next - y_prev
            rough[q, rows, :] = value
            hi, lo = split(value)
            base = i * chunk
            cols = slice(128 * q, 128 * q + 128)
            rcat[pl.ds(pl.multiple_of(base, chunk), chunk), cols] = hi
            rcat[pl.ds(pl.multiple_of(base + KP, chunk), chunk), cols] = lo
            rcat[pl.ds(pl.multiple_of(base + 2 * KP, chunk), chunk), cols] = hi
        return 0

    lax.fori_loop(0, chunks, rough_rows, 0)

    def mix_region(r, _):
        rows = pl.ds(pl.multiple_of(r * ROWS, 32), ROWS)
        pmix[rows, :] = jnp.dot(acat[rows, :], rcat[...], preferred_element_type=F32)
        return 0

    lax.fori_loop(0, NREG, mix_region, 0)

    await_all(1, uc)
    zones = [uc[q, GRP : GRP + 1, :] for q in range(4)]
    avgs = [vc[q, GRP : GRP + 1, :] for q in range(4)]

    def relax_rows(i, _):
        rows = chunk_of(i)
        for q in range(4):
            cols = slice(128 * q, 128 * q + 128)
            part = [
                pmix[pl.ds(pl.multiple_of(r * ROWS + i * chunk, chunk), chunk), cols]
                for r in range(NREG)
            ]
            mixed = part[3]
            for r in range(3):
                mixed = jnp.where(zones[q] == float(r), part[r], mixed)
            rel[q, rows, :] = uc[q, rows, :] - MIX * (rough[q, rows, :] + mixed)
        return 0

    lax.fori_loop(0, chunks, relax_rows, 0)
    exchange_x(4, rel, hxr)
    pack(rel, pkr)
    exchange_y(6, pkr, hyr)
    send_to(2, st, slot(tc, p, m, GRP), late)
    send_out(3, rel, ro, False)
    send_out(3, rel, ro, True)

    def put_grad(i, col, value):
        hi, lo = split(value)
        base = i * chunk
        cols = slice(col, col + 128)
        gcat[pl.ds(pl.multiple_of(base, chunk), chunk), cols] = hi
        gcat[pl.ds(pl.multiple_of(base + KP, chunk), chunk), cols] = lo
        gcat[pl.ds(pl.multiple_of(base + 2 * KP, chunk), chunk), cols] = hi

    def grad_z(i, _):
        rows = chunk_of(i)
        for q in range(4):
            z_next, z_prev = z_pair(rel[q, rows, :])
            put_grad(i, 1024 + 128 * q, z_next - z_prev)
        return 0

    lax.fori_loop(0, chunks, grad_z, 0)

    def at_points(col, half):
        cols = pl.ds(pl.multiple_of(col + half * 256, 256), 256)
        return jnp.dot(bcat[...], gcat[:, cols], preferred_element_type=F32)

    def half_cols(half):
        return pl.ds(pl.multiple_of(half * 256, 256), 256)

    def points_z(half, _):
        g = at_points(1024, half)
        jsum[:, half_cols(half)] = g * g
        return 0

    lax.fori_loop(0, 2, points_z, 0)

    await_halo(4, hxr.at[0])
    await_halo(5, hxr.at[1])
    await_halo(6, hyr.at[0])
    await_halo(7, hyr.at[1])

    def grad_xy(i, _):
        rows = chunk_of(i)
        edges = edges_of(hyr, i)
        for q in range(4):
            y_next, y_prev = y_pair(rel[q, rows, :], edges[q])
            x_next, x_prev = x_pair(rel, hxr, q, rows)
            put_grad(i, 128 * q, x_next - x_prev)
            put_grad(i, 512 + 128 * q, y_next - y_prev)
        return 0

    lax.fori_loop(0, chunks, grad_xy, 0)

    def points_xy(half, _):
        cols = half_cols(half)
        g = at_points(0, half)
        jsum[:, cols] = jsum[:, cols] + g * g
        g = at_points(512, half)
        jsum[:, cols] = jsum[:, cols] + g * g
        return 0

    lax.fori_loop(0, 2, points_xy, 0)

    await_all(2, tc)
    exchange_x(8, tc, hxt)

    def joule_rows(i, _):
        rows = chunk_of(i)
        for q in range(4):
            gain = lift[3, rows, :]
            for r in range(3):
                gain = jnp.where(zones[q] == float(r), lift[r, rows, :], gain)
            cols = slice(128 * q, 128 * q + 128)
            hi, lo = split(jsum[rows, cols] * gain)
            base = i * chunk
            jcat[pl.ds(pl.multiple_of(base, chunk), chunk), cols] = hi
            jcat[pl.ds(pl.multiple_of(base + NQ, chunk), chunk), cols] = lo
            jcat[pl.ds(pl.multiple_of(base + 2 * NQ, chunk), chunk), cols] = hi
        return 0

    lax.fori_loop(0, NQ // chunk, joule_rows, 0)

    def heat_half(half, _):
        cols = half_cols(half)
        pmix[0:ROWS, cols] = jnp.dot(wcat[...], jcat[:, cols], preferred_element_type=F32)
        return 0

    lax.fori_loop(0, 2, heat_half, 0)
    def adv_rows(outer):
        def body(i, _):
            rows = chunk_of(i)
            for q in (0, 3) if outer else (1, 2):
                t_next, t_prev = x_pair(tc, hxt, q, rows)
                scale = avgs[q] * 0.025
                adv[q, rows, :] = (
                    pmix[rows, 128 * q : 128 * q + 128] * scale + 0.15 * (t_next + t_prev)
                )
            return 0

        lax.fori_loop(0, chunks, body, 0)

    adv_rows(False)
    send_out(4, adv, ao, False)
    await_halo(8, hxt.at[0])
    await_halo(9, hxt.at[1])
    adv_rows(True)
    send_out(4, adv, ao, True)

    def tfix_block(bb, _):
        cur = st[bb]
        before = st[jnp.maximum(bb - 1, 0)] * (bb > 0).astype(F32)
        after = st[jnp.minimum(bb + 1, 15)] * (bb < 15).astype(F32)
        y_next = jnp.where(high8, pltpu.roll(after, 120, 1), pltpu.roll(cur, 120, 1))
        y_prev = jnp.where(low8, pltpu.roll(before, 8, 1), pltpu.roll(cur, 8, 1))
        z_next = jnp.where(z_has_next, pltpu.roll(cur, 127, 1), 0.0)
        z_prev = jnp.where(z_has_prev, pltpu.roll(cur, 1, 1), 0.0)
        tfix[bb] = cur - 0.15 * (6.0 * cur - y_next - y_prev - z_next - z_prev)
        return 0

    lax.fori_loop(0, 16, tfix_block, 0)

    local = pltpu.make_async_copy(tfix, tfix_out, in_sem.at[0])
    local.start()
    await_all(3, ro)
    for bb in range(16):
        v_ref[pl.ds(bb, GRP, stride=16), :] = ro[bb, 0:GRP]
    final = pltpu.make_async_copy(v_ref, rel_out, in_sem.at[1])
    final.start()
    for f in range(4):
        await_sent(f, sv)
    for j in (0, 1, 4, 5, 8, 9):
        await_halo_sent(j, hxv.at[0])
    for j in (2, 3, 6, 7):
        await_halo_sent(j, pkr.at[0])
    local.wait()
    final.wait()
    await_sent(4, sv)
    await_all(4, ao)


def assemble(rel, ao, tfix, rel_out, adv_out, adv, sem):
    first = pltpu.make_async_copy(rel, rel_out, sem.at[0])
    first.start()
    for bb in range(16):
        adv[pl.ds(bb, GRP, stride=16), :] = ao[bb, 0:GRP] + tfix[bb, 0:GRP]
    second = pltpu.make_async_copy(adv, adv_out, sem.at[1])
    second.start()
    first.wait()
    second.wait()


def on_device(v, i, t, avg, zone, zrr, exps, choice, share):
    flat = lambda x: x.reshape(GRP * 16, 128)
    vmem = pl.BlockSpec(memory_space=pltpu.VMEM)
    hbm = pl.BlockSpec(memory_space=pltpu.HBM)
    free = pl.BlockSpec(memory_space=pl.ANY)
    field = pltpu.VMEM((4, ROWS, 128), F32)
    blocks = pltpu.VMEM((16, SLOT, 128), F32)
    pair = pltpu.VMEM((2, ROWS, 128), F32)
    flats = pltpu.VMEM((GRP * 16, 128), F32)
    packed = pltpu.VMEM((2, ROWS // 4, 128), F32)
    parts = pl.pallas_call(
        kernel,
        out_shape=[jax.ShapeDtypeStruct((GRP * 16, 128), F32)]
        + [jax.ShapeDtypeStruct((16, SLOT, 128), F32)] * 2,
        in_specs=[hbm] * 9,
        out_specs=[free] * 3,
        scratch_shapes=[
            flats, flats, flats,
            pltpu.VMEM((16, 128), F32),
            pltpu.VMEM((16, 128), jnp.int32),
            pltpu.SMEM((NREG, NPAR), F32),
            pltpu.VMEM((NPAR, NMODE), jnp.int32),
            pltpu.VMEM((NPAR, NQ), jnp.int32),
            pltpu.VMEM((1, NQ), jnp.int32),
            blocks, blocks, blocks, blocks,
            field, field, field, field, field, field, blocks,
            pair, packed, pair, packed, pair,
            packed, packed,
            pltpu.VMEM((128, 512), F32),
            pltpu.VMEM((256, 128), F32),
            pltpu.VMEM((16, 256), F32),
            pltpu.VMEM((3, 16, NQ), F32),
            pltpu.VMEM((NQ, 128), F32),
            pltpu.VMEM((KP, NQ), F32),
            pltpu.VMEM((NREG * ROWS, 3 * KP), BF16),
            pltpu.VMEM((NQ, 3 * KP), BF16),
            pltpu.VMEM((ROWS, 3 * NQ), BF16),
            pltpu.VMEM((3 * KP, 512), BF16),
            pltpu.VMEM((NREG * ROWS, 512), F32),
            pltpu.VMEM((3 * KP, 3 * 512), BF16),
            pltpu.VMEM((NQ, 512), F32),
            pltpu.VMEM((3 * NQ, 512), BF16),
            pltpu.VMEM((NREG, NQ, 128), F32),
            pltpu.SemaphoreType.DMA((9,)),
            pltpu.SemaphoreType.DMA((5,)),
            pltpu.SemaphoreType.DMA((5,)),
            pltpu.SemaphoreType.DMA((10,)),
            pltpu.SemaphoreType.DMA((10,)),
        ],
        compiler_params=pltpu.CompilerParams(
            collective_id=0, has_side_effects=True, vmem_limit_bytes=36 << 20
        ),
        name="step",
    )(*(
        pltpu.with_memory_space_constraint(x, pltpu.HBM)
        for x in (
            flat(v), flat(i), flat(t), avg.reshape(16, 128), zone.reshape(16, 128), zrr,
            exps.T, choice.T, share.reshape(1, NQ),
        )
    ))
    rel, adv = pl.pallas_call(
        assemble,
        out_shape=[jax.ShapeDtypeStruct((GRP * 16, 128), F32)] * 2,
        in_specs=[free, vmem, vmem],
        out_specs=[free] * 2,
        scratch_shapes=[flats, pltpu.SemaphoreType.DMA((2,))],
        compiler_params=pltpu.CompilerParams(vmem_limit_bytes=16 << 20),
        name="assemble",
    )(*parts)
    shape = (GRP, 1, 2048)
    return rel.reshape(shape), adv.reshape(shape)


def solution(mesh):
    field = P("modes", "space", None)
    cells = P("space", None)
    return jax.shard_map(
        on_device,
        mesh=mesh,
        in_specs=(field, field, field, cells, cells, P(), P(), P(), P()),
        out_specs=(field, field),
        check_vma=False,
    )
```
